32 devices in a mesh: slab: 32 (over z, y, x, core).
Axes of the slice: x: 2, y: 2, z: 4, core: 2. Of those that a mesh axis runs over, the one named last changes fastest.
Arguments:
- series: float32 [80, 1048576], P(None, 'slab'), as said below
- noise_mask: int32 [1048576], P('slab'), may hold values 0 or 1
- probes: float32 [80, 5], replicated, may hold values from -6 to 6
- sample_weights: bfloat16 [1536, 256, 128], P('slab'), may hold values from -0.375 to 0.375
- block_ids: int32 [1536], P('slab'), may hold values from 0 to 127
- tile_ids: int32 [1536], P('slab'), may hold values from -1 to 127, as said below
- tile_owner: int32 [128], replicated, may hold values from 0 to 31, as said below
Outputs:
- vertex_series: float32 [128, 80, 128], P('slab')
The draws below stay inside these ranges and needn't reach their ends.
Inputs may be any that keep to these rules, and one draw needn't show every extreme that they name: `tile_ids`: on each device the used entries come first and are at least half of its 48 entries; some device uses all. Used entry k of the device with index d names vertex tile (d * 4 + o_d + k) mod 128, with o_d in [0, 4) fixed per device; unused entries hold -1. tile_owner[j] = p[j mod the number of devices] for a permutation p of the devices, so every device owns 4 tiles. `series`: values of order one to some tens; each voxel carries its own baseline.
All inputs are finite; a program needn't handle non-finite values. No bound on the sum of `noise_mask` on one device may be relied on, other than what follows from the above.
Results may differ from the reference program's by a relative error of at most 0.005.
Values may be sent and summed in bfloat16 or wider, within the bound.
No kernel may reach another device: no remote copies, remote signals or barrier semaphores. Data moves between devices by JAX's collectives and lax.ppermute only.
A program may use at most 128 MiB of HBM per device.

```python
import jax
import jax.numpy as jnp
from jax import lax

FRAMES = 80
COMPS = 5
VOXBLK = 256
TILE = 128
OWN = 4
BLK_DEV = 128
VOX_DEV = 32768
VOXELS = 1048576
VTILES = 128
ENT_DEV = 48
ENTRIES = 1536
N_SLAB = 32


def draw_series(key, part):
    keys = jax.random.split(key, 4)
    position = jnp.arange(VOXELS, dtype=jnp.float32) / VOXELS
    latent = jax.random.normal(keys[0], (8, FRAMES), jnp.float32)
    loading = jax.random.normal(keys[1], (8, VOXELS), jnp.float32)
    noise = jax.random.normal(keys[2], (FRAMES, VOXELS), jnp.float32)
    base = jax.random.uniform(keys[3], (1, VOXELS), jnp.float32, 0.0, 4.0)
    total = noise + base
    for index in range(8):
        bump = jnp.cos(3.14159265 * (3.0 * position + index / 8.0)) ** 2
        scale = 0.6 * 3.0 ** position * (0.3 + 2.0 * bump)
        total = total + latent[index][:, None] * (loading[index] * scale)[None, :]
    return total


def draw_tile_ids(key, part):
    keys = jax.random.split(jax.random.fold_in(key, 11), 3)
    index = jnp.arange(ENTRIES, dtype=jnp.int32)
    device = index // ENT_DEV
    entry = index % ENT_DEV
    offset = jax.random.randint(keys[0], (N_SLAB,), 0, OWN, jnp.int32)
    used = jax.random.randint(keys[1], (N_SLAB,), ENT_DEV // 2, ENT_DEV + 1, jnp.int32)
    fullest = jax.random.randint(keys[2], (), 0, N_SLAB, jnp.int32)
    used = jnp.where(jnp.arange(N_SLAB, dtype=jnp.int32) == fullest, ENT_DEV, used)
    tiles = (device * OWN + offset[device] + entry) % VTILES
    return jnp.where(entry < used[device], tiles, -1).astype(jnp.int32)


def draw_tile_owner(key, part):
    order = jax.random.permutation(jax.random.fold_in(key, 23), N_SLAB).astype(jnp.int32)
    return order[jnp.arange(VTILES, dtype=jnp.int32) % N_SLAB]


def plant(values, own_key, low, high):
    shape = values.shape
    index_at = [jax.random.randint(jax.random.fold_in(own_key, axis), (), 0, shape[axis]) for axis in range(len(shape))]
    values = values.at[tuple(index_at)].set(low)
    longest = shape.index(max(shape))
    index_at[longest] = (index_at[longest] + 1) % shape[longest]
    return values.at[tuple(index_at)].set(high)


def shard_levels(own_key, shape, shards, low, largest):
    def one(dim, shards_of):
        steps = jax.random.uniform(jax.random.fold_in(jax.random.fold_in(own_key, 6), dim), (shards_of,), jnp.float32, low / len(shards), largest / len(shards))
        return jnp.repeat(jnp.exp(steps), shape[dim] // shards_of).reshape((-1,) + (1,) * (len(shape) - dim - 1))

    factor_of = one(*shards[0])
    for cut in shards[1:]:
        factor_of = factor_of * one(*cut)
    return factor_of


def scatter_about(rng, dims, deviation, reach, cuts=(), held_as=jnp.bfloat16):
    drawn = jax.random.normal(rng, dims, jnp.float32) * deviation
    if len(cuts) > 0:
        drawn = shard_levels(rng, dims, cuts, -0.22, 0.18) * drawn
    return jnp.clip(drawn, min=-reach, max=reach).astype(held_as)


def setup_inputs(seed: int = 0) -> dict:
    splits = jax.random.split(jax.random.key(seed), 8)
    series = draw_series(jax.random.fold_in(splits[7], 71), 0)
    noise_mask = plant((jax.random.randint(splits[1], (VOXELS,), 0, 4) < 1).astype(jnp.int32), jax.random.fold_in(splits[1], 1), 0, 1)
    probes = scatter_about(splits[2], (FRAMES, COMPS), 1.0, 6.0, (), jnp.float32)
    sample_weights = scatter_about(splits[3], (ENTRIES, VOXBLK, TILE), VOXBLK ** -0.5, 0.375, ((0, 32),))
    block_ids = plant(jax.random.randint(splits[4], (ENTRIES,), 0, BLK_DEV), jax.random.fold_in(splits[4], 1), 0, BLK_DEV - 1).astype(jnp.int32)
    tile_ids = draw_tile_ids(jax.random.fold_in(splits[7], 71), 0)
    tile_owner = draw_tile_owner(jax.random.fold_in(splits[7], 71), 0)
    return {"series": series, "noise_mask": noise_mask, "probes": probes, "sample_weights": sample_weights, "block_ids": block_ids, "tile_ids": tile_ids, "tile_owner": tile_owner}


HIGHEST = lax.Precision.HIGHEST

def make_projector(components):
    inner = jnp.dot(components.T, components, precision=HIGHEST)
    factor = jnp.linalg.cholesky(inner)
    solved = jax.scipy.linalg.cho_solve((factor, True), components.T)
    return jnp.dot(components, solved, precision=HIGHEST)

def reference(series, noise_mask, probes, sample_weights, block_ids, tile_ids, tile_owner):
    demeaned = series - jnp.mean(series, axis=0, keepdims=True)
    weighted = demeaned * noise_mask.astype(jnp.float32)[None, :]
    noise_gram = lax.dot_general(weighted, demeaned, (((1,), (1,)), ((), ())), precision=HIGHEST)
    components = jnp.dot(noise_gram, probes, precision=HIGHEST)
    projector = make_projector(components)

    def one_device(accum, device):
        columns = lax.dynamic_slice_in_dim(demeaned, (device * VOX_DEV).astype(jnp.int32), VOX_DEV, 1)
        cleaned = (columns - jnp.dot(projector, columns, precision=HIGHEST)).astype(jnp.bfloat16)
        blocks = cleaned.reshape(FRAMES, BLK_DEV, VOXBLK)
        first = (device * ENT_DEV).astype(jnp.int32)
        chosen = lax.dynamic_slice_in_dim(block_ids, first, ENT_DEV, 0)
        tiles = lax.dynamic_slice_in_dim(tile_ids, first, ENT_DEV, 0)
        weights = lax.dynamic_slice_in_dim(sample_weights, first, ENT_DEV, 0)
        picked = jnp.take(blocks, chosen, axis=1)
        partial_value = jnp.einsum('fkv,kvt->kft', picked.astype(jnp.float32), weights.astype(jnp.float32)).astype(jnp.bfloat16)
        owners = tile_owner[jnp.maximum(tiles, 0)]
        rows = jnp.where(tiles >= 0, owners * OWN + tiles // N_SLAB, VTILES).astype(jnp.int32)
        accum = accum.at[rows].add(partial_value.astype(jnp.float32), mode='drop')
        return (accum, None)
    start = jnp.zeros((VTILES, FRAMES, TILE), jnp.float32)
    result, unused = lax.scan(one_device, start, jnp.arange(N_SLAB, dtype=jnp.int32))
    return result
```

```python
import functools

import jax
import jax.numpy as jnp
from jax import lax
from jax.experimental import pallas as pl
from jax.experimental.pallas import tpu as pltpu
from jax.sharding import PartitionSpec as P

AXIS = "slab"
HIGHEST = lax.Precision.HIGHEST
LANES = 128
COEF_ROWS = 8
STEP_BLOCKS = 8


class Plan:
    def __init__(self, devices, tiles, entries, frames, block_width, tile_width):
        self.devices = devices
        self.tiles = tiles
        self.entries = entries
        self.frames = frames
        self.block_width = block_width
        self.tile_width = tile_width
        self.owned = tiles // devices
        self.log = devices.bit_length() - 1
        assert 1 << self.log == devices and self.owned * devices == tiles
        widths = [1]
        while sum(widths) < self.log:
            widths.append(min(2, self.log - sum(widths)))
        self.widths = widths
        self.done = [sum(widths[:i]) for i in range(len(widths) + 1)]
        self.slots = [
            min(self.owned, -(-(self.owned * (1 << b) + entries - 1) // devices))
            for b in self.done
        ]
        self.slots[-1] = self.owned
        self.owners = [devices >> self.done[i + 1] for i in range(len(widths))]

    def rows(self, stage):
        return self.owners[stage] * self.slots[stage] * self.frames + COEF_ROWS

    def position(self, rel, stage):
        place = 0
        for i in range(stage, len(self.widths)):
            digit = (rel >> self.done[i]) & ((1 << self.widths[i]) - 1)
            place = (place << self.widths[i]) | digit
        return place

    def relative(self, place, stage):
        rel = 0
        for i in reversed(range(stage, len(self.widths))):
            rel = rel | ((place & ((1 << self.widths[i]) - 1)) << self.done[i])
            place = place >> self.widths[i]
        return rel


def tile_rows(index, frames):
    return pl.ds(pl.multiple_of(index * frames, 8), frames)


def sample_kernel(
    plan, steps, block_ids, tile_ids, tile_owner, series, mask, probes, weights,
    keep, send, inverse, halves, masked, gram, held, semaphore,
):
    step = pl.program_id(0)
    frames, width = plan.frames, plan.block_width
    columns = series.shape[1]
    weights_copy = pltpu.make_async_copy(weights, held, semaphore)

    @pl.when(step == 0)
    def _():
        weights_copy.start()
        gram[...] = jnp.zeros_like(gram)
        keep[...] = jnp.zeros_like(keep)
        send[...] = jnp.zeros_like(send)

        def note(residue, carry):
            inverse[tile_owner[residue]] = residue
            return carry

        lax.fori_loop(0, plan.devices, note, 0)

    start = step * columns
    for block in range(columns // width):
        place = pl.ds(block * width, width)
        values = series[:, place]
        values = values - jnp.sum(values, axis=0, keepdims=True) * (1.0 / frames)
        high = values.astype(jnp.bfloat16)
        low = (values - high.astype(jnp.float32)).astype(jnp.bfloat16)
        used = mask[:, place].astype(jnp.float32).astype(jnp.bfloat16)
        target = pl.ds(pl.multiple_of(start + block * width, width), width)
        halves[0:frames, target] = high
        halves[frames:, target] = low
        masked[0:frames, place] = high * used
        masked[frames:, place] = low * used
    gram[...] += lax.dot_general(
        masked[...],
        halves[:, pl.ds(pl.multiple_of(start, width), columns)],
        (((1,), (1,)), ((), ())),
        preferred_element_type=jnp.float32,
    )

    @pl.when(step == steps - 1)
    def _():
        device = lax.axis_index(AXIS)
        full = gram[0:frames, 0:frames] + gram[frames:, frames:]
        full = full + gram[0:frames, frames:] + gram[frames:, 0:frames]
        coefs = jnp.dot(
            probes[...], full, precision=HIGHEST, preferred_element_type=jnp.float32
        )
        last = keep.shape[0] - COEF_ROWS
        for out in (keep, send):
            out[pl.ds(last, COEF_ROWS), 0:frames] = coefs
        weights_copy.wait()

        def entry(k, carry):
            tile = tile_ids[k]

            @pl.when(tile >= 0)
            def _():
                columns_of = pl.ds(pl.multiple_of(block_ids[k] * width, width), width)
                both = jnp.dot(
                    halves[:, columns_of], held[k], preferred_element_type=jnp.float32
                )
                total = both[0:frames] + both[frames:]
                rel = tile_owner[tile & (plan.devices - 1)] ^ device
                offset = (tile - device * plan.owned) & (plan.tiles - 1)
                slot = plan.position(rel, 1) * plan.slots[0] + (offset >> plan.log)
                target = tile_rows(slot, frames)

                @pl.when((rel & 1) == 0)
                def _():
                    keep[target, :] = total

                @pl.when((rel & 1) == 1)
                def _():
                    send[target, :] = total

            return carry

        lax.fori_loop(0, plan.entries, entry, 0)


def sample(plan, series, mask, probes, weights, block_ids, tile_ids, tile_owner):
    frames, voxels = series.shape
    columns = STEP_BLOCKS * plan.block_width
    steps = voxels // columns
    smem = pl.BlockSpec(memory_space=pltpu.SMEM)
    block = jax.ShapeDtypeStruct((plan.rows(0), LANES), jnp.float32)
    whole = pl.BlockSpec(block.shape, lambda i: (0, 0), pipeline_mode=pl.Buffered(1))
    return pl.pallas_call(
        functools.partial(sample_kernel, plan, steps),
        name="sample",
        grid=(steps,),
        in_specs=[
            smem,
            smem,
            smem,
            pl.BlockSpec((frames, columns), lambda i: (0, i)),
            pl.BlockSpec((1, columns), lambda i: (0, i)),
            pl.BlockSpec(probes.shape, lambda i: (0, 0)),
            pl.BlockSpec(memory_space=pl.ANY),
        ],
        out_specs=[whole, whole, smem],
        out_shape=[block, block, jax.ShapeDtypeStruct((plan.devices,), jnp.int32)],
        scratch_shapes=[
            pltpu.VMEM((2 * frames, voxels), jnp.bfloat16),
            pltpu.VMEM((2 * frames, columns), jnp.bfloat16),
            pltpu.VMEM((2 * frames, 2 * frames), jnp.float32),
            pltpu.VMEM(weights.shape, weights.dtype),
            pltpu.SemaphoreType.DMA,
        ],
        compiler_params=pltpu.CompilerParams(
            dimension_semantics=("arbitrary",), vmem_limit_bytes=56 << 20
        ),
    )(block_ids, tile_ids, tile_owner, series, mask, probes, weights)


def add_tiles(plan, stage, inverse, sources, place, slot):
    device = lax.axis_index(AXIS)
    done, after = plan.done[stage], plan.done[stage + 1]
    slots, devices, tiles = plan.slots[stage], plan.devices, plan.tiles
    residue = inverse[device ^ plan.relative(place, stage + 1)]
    last = stage + 1 == len(plan.widths)
    base = 0 if last else ((device >> after) << after) * plan.owned
    tile = (base + ((residue - base) & (devices - 1)) + slot * devices) & (tiles - 1)
    total = None
    for digit, source in enumerate(sources):
        sender = device ^ (digit << done)
        first = ((sender >> done) << done) * plan.owned
        offset = (tile - first) & (tiles - 1)
        there = offset < slots * devices
        at = place * slots + jnp.minimum(offset >> plan.log, slots - 1)
        value = source[tile_rows(at, plan.frames), :]
        value = jnp.where(there, value, 0.0)
        total = value if total is None else total + value
    return total


def add_coefs(sources):
    total = None
    for source in sources:
        value = source[pl.ds(source.shape[0] - COEF_ROWS, COEF_ROWS), :]
        total = value if total is None else total + value
    return total


def merge_kernel(plan, stage, inverse, *refs):
    fan = 1 << plan.widths[stage]
    sources, outs = refs[:fan], refs[fan:]
    coefs = add_coefs(sources)
    slots, count = plan.slots[stage + 1], plan.owners[stage + 1]
    for digit, out in enumerate(outs):
        out[pl.ds(out.shape[0] - COEF_ROWS, COEF_ROWS), :] = coefs

        def owner(rest, carry):
            for slot in range(slots):
                value = add_tiles(plan, stage, inverse, sources, digit * count + rest, slot)
                out[tile_rows(rest * slots + slot, plan.frames), :] = value
            return carry

        if count <= 4:
            for rest in range(count):
                owner(rest, 0)
        else:
            lax.fori_loop(0, count, owner, 0)


def merge(plan, stage, inverse, sources):
    fan = 1 << plan.widths[stage + 1]
    block = jax.ShapeDtypeStruct((plan.rows(stage + 1), LANES), jnp.float32)
    vmem = pl.BlockSpec(memory_space=pltpu.VMEM)
    return pl.pallas_call(
        functools.partial(merge_kernel, plan, stage),
        name="merge",
        in_specs=[pl.BlockSpec(memory_space=pltpu.SMEM)] + [vmem] * len(sources),
        out_specs=[vmem] * fan,
        out_shape=[block] * fan,
        compiler_params=pltpu.CompilerParams(vmem_limit_bytes=40 << 20),
    )(inverse, *sources)


def finish_kernel(plan, comps, inverse, *refs):
    stage = len(plan.widths) - 1
    sources, out = refs[:-1], refs[-1]
    frames = plan.frames
    basis = add_coefs(sources)
    lane = lax.broadcasted_iota(jnp.int32, basis.shape, 1)
    row = lax.broadcasted_iota(jnp.int32, basis.shape, 0)
    basis = jnp.where((lane < frames) & (row < comps), basis, 0.0)
    unit = jnp.zeros_like(basis)
    for i in range(comps):
        line = basis[i : i + 1, :]
        line = line * lax.rsqrt(jnp.sum(line * line, axis=1, keepdims=True))
        unit = jnp.where(row == i, line, unit)
        basis = basis - jnp.sum(basis * line, axis=1, keepdims=True) * line
    unit = unit[:, 0:frames]
    for slot in range(plan.owned):
        value = add_tiles(plan, stage, inverse, sources, 0, slot)
        along = jnp.dot(unit, value, precision=HIGHEST, preferred_element_type=jnp.float32)
        out[slot] = value - lax.dot_general(
            unit,
            along,
            (((0,), (0,)), ((), ())),
            precision=HIGHEST,
            preferred_element_type=jnp.float32,
        )


def finish(plan, comps, inverse, sources):
    vmem = pl.BlockSpec(memory_space=pltpu.VMEM)
    return pl.pallas_call(
        functools.partial(finish_kernel, plan, comps),
        name="finish",
        in_specs=[pl.BlockSpec(memory_space=pltpu.SMEM)] + [vmem] * len(sources),
        out_specs=vmem,
        out_shape=jax.ShapeDtypeStruct((plan.owned, plan.frames, plan.tile_width), jnp.float32),
    )(inverse, *sources)


def exchange(plan, stage, blocks):
    received = [blocks[0]]
    for digit in range(1, len(blocks)):
        pairs = [(i, i ^ (digit << plan.done[stage])) for i in range(plan.devices)]
        received.append(lax.ppermute(blocks[digit], AXIS, pairs))
    return received


def body(series, noise_mask, probes, sample_weights, block_ids, tile_ids, tile_owner):
    frames, voxels = series.shape
    entries, block_width, tile_width = sample_weights.shape
    plan = Plan(
        lax.axis_size(AXIS), tile_owner.shape[0], entries, frames, block_width, tile_width
    )
    comps = probes.shape[1]
    rows = jnp.pad(probes.T, ((0, COEF_ROWS - comps), (0, 0)))
    keep, send, inverse = sample(
        plan, series, noise_mask.reshape(1, voxels), rows, sample_weights,
        block_ids, tile_ids, tile_owner,
    )
    blocks = [keep, send]
    for stage in range(len(plan.widths)):
        blocks = exchange(plan, stage, blocks)
        if stage + 1 < len(plan.widths):
            blocks = merge(plan, stage, inverse, blocks)
    return finish(plan, comps, inverse, blocks)


def solution(mesh):
    return jax.shard_map(
        body,
        mesh=mesh,
        in_specs=(
            P(None, AXIS),
            P(AXIS),
            P(),
            P(AXIS, None, None),
            P(AXIS),
            P(AXIS),
            P(),
        ),
        out_specs=P(AXIS, None, None),
        check_vma=False,
    )
```

```python
import functools

import jax
import jax.numpy as jnp
from jax import lax
from jax.experimental import pallas as pl
from jax.experimental.pallas import tpu as pltpu
from jax.sharding import PartitionSpec as P

AXIS = "slab"
HIGHEST = lax.Precision.HIGHEST
LANES = 128
COEF_ROWS = 8
GROUP = 8
WIDE = 256
COEF_STEPS = 4
SAMPLE_VMEM = 56 << 20
COEF_VMEM = 40 << 20


class Plan:
    def __init__(self, devices, tiles, entries, frames, block_width, tile_width):
        self.devices = devices
        self.tiles = tiles
        self.entries = entries
        self.frames = frames
        self.block_width = block_width
        self.tile_width = tile_width
        self.owned = tiles // devices
        self.log = devices.bit_length() - 1
        assert 1 << self.log == devices and self.owned * devices == tiles
        widths = [1]
        while sum(widths) < self.log:
            widths.append(min(2, self.log - sum(widths)))
        self.widths = widths
        self.done = [sum(widths[:i]) for i in range(len(widths) + 1)]
        self.slots = [
            min(self.owned, -(-(self.owned * (1 << b) + entries - 1) // devices))
            for b in self.done
        ]
        self.slots[-1] = self.owned
        self.owners = [devices >> self.done[i + 1] for i in range(len(widths))]

    def rows(self, stage):
        return self.owners[stage] * self.slots[stage] * self.frames

    def position(self, rel, stage):
        place = 0
        for i in range(stage, len(self.widths)):
            digit = (rel >> self.done[i]) & ((1 << self.widths[i]) - 1)
            place = (place << self.widths[i]) | digit
        return place

    def relative(self, place, stage):
        rel = 0
        for i in reversed(range(stage, len(self.widths))):
            rel = rel | ((place & ((1 << self.widths[i]) - 1)) << self.done[i])
            place = place >> self.widths[i]
        return rel


def tile_rows(index, frames):
    return pl.ds(pl.multiple_of(index * frames, 8), frames)


def split(values):
    high = values.astype(jnp.bfloat16)
    low = (values - high.astype(jnp.float32)).astype(jnp.bfloat16)
    return high, low


def demean(values):
    return values - jnp.sum(values, axis=0, keepdims=True) * (1.0 / values.shape[0])


def sample_kernel(
    plan, block_ids, tile_ids, tile_owner, series, weights,
    keep, send, inverse, picked, held, pick_sems, weight_sems,
):
    frames, width = plan.frames, plan.block_width
    groups = plan.entries // GROUP

    def pick(k):
        start = pl.multiple_of(block_ids[k] * width, width)
        return pltpu.make_async_copy(
            series.at[:, pl.ds(start, width)], picked.at[k], pick_sems.at[k]
        )

    def fetch(g):
        span = pl.ds(g * GROUP, GROUP)
        return pltpu.make_async_copy(weights.at[span], held.at[span], weight_sems.at[g])

    def begin(g, carry):
        fetch(g).start()
        for i in range(GROUP):
            pick(g * GROUP + i).start()
        return carry

    lax.fori_loop(0, groups, begin, 0)
    keep[...] = jnp.zeros_like(keep)
    send[...] = jnp.zeros_like(send)
    for residue in range(plan.devices):
        inverse[tile_owner[residue]] = residue
    device = lax.axis_index(AXIS)
    spare = plan.owners[0] * plan.slots[0]

    def group(g, carry):
        fetch(g).wait()
        for i in range(GROUP):
            pick(g * GROUP + i).wait()
        for i in range(GROUP):
            k = g * GROUP + i
            tile = tile_ids[k]
            high, low = split(demean(picked[k]))
            both = jnp.dot(
                jnp.concatenate([high, low], axis=0),
                held[k],
                preferred_element_type=jnp.float32,
            )
            total = both[0:frames] + both[frames:]
            rel = tile_owner[tile & (plan.devices - 1)] ^ device
            offset = (tile - device * plan.owned) & (plan.tiles - 1)
            slot = plan.position(rel, 1) * plan.slots[0] + (offset >> plan.log)
            mine = (rel & 1) == 0
            used = tile >= 0
            to_keep = jnp.where(used & mine, slot, spare)
            to_send = jnp.where(used & jnp.logical_not(mine), slot, spare)
            keep[tile_rows(to_keep, frames), :] = total
            send[tile_rows(to_send, frames), :] = total
        return carry

    lax.fori_loop(0, groups, group, 0)


def sample(plan, series, weights, block_ids, tile_ids, tile_owner):
    frames, width = plan.frames, plan.block_width
    smem = pl.BlockSpec(memory_space=pltpu.SMEM)
    vmem = pl.BlockSpec(memory_space=pltpu.VMEM)
    hbm = pl.BlockSpec(memory_space=pl.ANY)
    block = jax.ShapeDtypeStruct((plan.rows(0) + frames, LANES), jnp.float32)
    return pl.pallas_call(
        functools.partial(sample_kernel, plan),
        name="sample",
        in_specs=[smem, smem, smem, hbm, hbm],
        out_specs=[vmem, vmem, smem],
        out_shape=[block, block, jax.ShapeDtypeStruct((plan.devices,), jnp.int32)],
        scratch_shapes=[
            pltpu.VMEM((plan.entries, frames, width), jnp.float32),
            pltpu.VMEM(weights.shape, weights.dtype),
            pltpu.SemaphoreType.DMA((plan.entries,)),
            pltpu.SemaphoreType.DMA((plan.entries // GROUP,)),
        ],
        compiler_params=pltpu.CompilerParams(vmem_limit_bytes=SAMPLE_VMEM),
    )(
        block_ids, tile_ids, tile_owner,
        pltpu.with_memory_space_constraint(series, pltpu.HBM),
        pltpu.with_memory_space_constraint(weights, pltpu.HBM),
    )


def coef_kernel(
    steps, series, mask, probes, coefs, held, marks, halves, masked, gram, sems, mark_sem
):
    frames = series.shape[0]
    columns = series.shape[1] // steps

    def fetch(step):
        span = pl.ds(pl.multiple_of(step * columns, columns), columns)
        return pltpu.make_async_copy(series.at[:, span], held.at[:, span], sems.at[step])

    mark_copy = pltpu.make_async_copy(mask, marks, mark_sem)
    mark_copy.start()
    for step in range(steps):
        fetch(step).start()
    gram[...] = jnp.zeros_like(gram)
    mark_copy.wait()

    def chunk(step, carry):
        fetch(step).wait()
        start = step * columns
        for at in range(0, columns, WIDE):
            span = pl.ds(pl.multiple_of(start + at, WIDE), WIDE)
            place = pl.ds(at, WIDE)
            high, low = split(demean(held[:, span]))
            used = marks[:, span].astype(jnp.float32).astype(jnp.bfloat16)
            halves[0:frames, place] = high
            halves[frames:, place] = low
            masked[0:frames, place] = high * used
            masked[frames:, place] = low * used
        gram[...] += lax.dot_general(
            masked[...],
            halves[...],
            (((1,), (1,)), ((), ())),
            preferred_element_type=jnp.float32,
        )
        return carry

    lax.fori_loop(0, steps, chunk, 0)
    full = gram[0:frames, 0:frames] + gram[frames:, frames:]
    full = full + gram[0:frames, frames:] + gram[frames:, 0:frames]
    coefs[...] = jnp.zeros_like(coefs)
    coefs[0 : probes.shape[0], 0:frames] = jnp.dot(
        probes[...], full, precision=HIGHEST, preferred_element_type=jnp.float32
    )


def local_coefs(series, noise_mask, probes):
    frames, voxels = series.shape
    columns = voxels // COEF_STEPS
    vmem = pl.BlockSpec(memory_space=pltpu.VMEM)
    hbm = pl.BlockSpec(memory_space=pl.ANY)
    return pl.pallas_call(
        functools.partial(coef_kernel, COEF_STEPS),
        name="coefs",
        in_specs=[hbm, hbm, vmem],
        out_specs=vmem,
        out_shape=jax.ShapeDtypeStruct((COEF_ROWS, LANES), jnp.float32),
        scratch_shapes=[
            pltpu.VMEM(series.shape, series.dtype),
            pltpu.VMEM((1, voxels), noise_mask.dtype),
            pltpu.VMEM((2 * frames, columns), jnp.bfloat16),
            pltpu.VMEM((2 * frames, columns), jnp.bfloat16),
            pltpu.VMEM((2 * frames, 2 * frames), jnp.float32),
            pltpu.SemaphoreType.DMA((COEF_STEPS,)),
            pltpu.SemaphoreType.DMA,
        ],
        compiler_params=pltpu.CompilerParams(vmem_limit_bytes=COEF_VMEM),
        cost_estimate=pl.CostEstimate(
            flops=8 * frames * frames * voxels,
            bytes_accessed=4 * frames * voxels,
            transcendentals=0,
        ),
    )(
        pltpu.with_memory_space_constraint(series, pltpu.HBM),
        pltpu.with_memory_space_constraint(noise_mask.reshape(1, voxels), pltpu.HBM),
        probes.T,
    )


def add_tiles(plan, stage, inverse, sources, place, slot):
    device = lax.axis_index(AXIS)
    done, after = plan.done[stage], plan.done[stage + 1]
    slots, devices, tiles = plan.slots[stage], plan.devices, plan.tiles
    residue = inverse[device ^ plan.relative(place, stage + 1)]
    last = stage + 1 == len(plan.widths)
    base = 0 if last else ((device >> after) << after) * plan.owned
    tile = (base + ((residue - base) & (devices - 1)) + slot * devices) & (tiles - 1)
    total = None
    for digit, source in enumerate(sources):
        sender = device ^ (digit << done)
        first = ((sender >> done) << done) * plan.owned
        offset = (tile - first) & (tiles - 1)
        there = offset < slots * devices
        at = place * slots + jnp.minimum(offset >> plan.log, slots - 1)
        value = source[tile_rows(at, plan.frames), :]
        value = jnp.where(there, value, 0.0)
        total = value if total is None else total + value
    return total


def merge_kernel(plan, stage, inverse, *refs):
    fan = 1 << plan.widths[stage]
    sources, outs = refs[:fan], refs[fan:]
    slots, count = plan.slots[stage + 1], plan.owners[stage + 1]
    for digit, out in enumerate(outs):

        def owner(rest, carry):
            for slot in range(slots):
                value = add_tiles(plan, stage, inverse, sources, digit * count + rest, slot)
                out[tile_rows(rest * slots + slot, plan.frames), :] = value
            return carry

        if count <= 4:
            for rest in range(count):
                owner(rest, 0)
        else:
            lax.fori_loop(0, count, owner, 0)


def merge(plan, stage, inverse, sources):
    fan = 1 << plan.widths[stage + 1]
    block = jax.ShapeDtypeStruct((plan.rows(stage + 1), LANES), jnp.float32)
    vmem = pl.BlockSpec(memory_space=pltpu.VMEM)
    return pl.pallas_call(
        functools.partial(merge_kernel, plan, stage),
        name="merge",
        in_specs=[pl.BlockSpec(memory_space=pltpu.SMEM)] + [vmem] * len(sources),
        out_specs=[vmem] * fan,
        out_shape=[block] * fan,
        compiler_params=pltpu.CompilerParams(vmem_limit_bytes=40 << 20),
    )(inverse, *sources)


def finish_kernel(plan, comps, inverse, coefs, *refs):
    stage = len(plan.widths) - 1
    sources, out = refs[:-1], refs[-1]
    frames = plan.frames
    basis = coefs[...]
    lane = lax.broadcasted_iota(jnp.int32, basis.shape, 1)
    row = lax.broadcasted_iota(jnp.int32, basis.shape, 0)
    basis = jnp.where((lane < frames) & (row < comps), basis, 0.0)
    unit = jnp.zeros_like(basis)
    for i in range(comps):
        line = basis[i : i + 1, :]
        line = line * lax.rsqrt(jnp.sum(line * line, axis=1, keepdims=True))
        unit = jnp.where(row == i, line, unit)
        basis = basis - jnp.sum(basis * line, axis=1, keepdims=True) * line
    unit = unit[:, 0:frames]
    for slot in range(plan.owned):
        value = add_tiles(plan, stage, inverse, sources, 0, slot)
        along = jnp.dot(unit, value, precision=HIGHEST, preferred_element_type=jnp.float32)
        out[slot] = value - lax.dot_general(
            unit,
            along,
            (((0,), (0,)), ((), ())),
            precision=HIGHEST,
            preferred_element_type=jnp.float32,
        )


def finish(plan, comps, inverse, coefs, sources):
    vmem = pl.BlockSpec(memory_space=pltpu.VMEM)
    return pl.pallas_call(
        functools.partial(finish_kernel, plan, comps),
        name="finish",
        in_specs=[pl.BlockSpec(memory_space=pltpu.SMEM)] + [vmem] * (1 + len(sources)),
        out_specs=vmem,
        out_shape=jax.ShapeDtypeStruct((plan.owned, plan.frames, plan.tile_width), jnp.float32),
    )(inverse, coefs, *sources)


def exchange(plan, stage, blocks):
    received = [blocks[0]]
    for digit in range(1, len(blocks)):
        pairs = [(i, i ^ (digit << plan.done[stage])) for i in range(plan.devices)]
        received.append(lax.ppermute(blocks[digit], AXIS, pairs))
    return received


def body(series, noise_mask, probes, sample_weights, block_ids, tile_ids, tile_owner):
    frames, voxels = series.shape
    entries, block_width, tile_width = sample_weights.shape
    plan = Plan(
        lax.axis_size(AXIS), tile_owner.shape[0], entries, frames, block_width, tile_width
    )
    keep, send, inverse = sample(
        plan, series, sample_weights, block_ids, tile_ids, tile_owner
    )
    blocks = exchange(plan, 0, [keep, send])
    blocks = merge(plan, 0, inverse, blocks)
    coefs = local_coefs(series, noise_mask, probes)
    for stage in range(len(plan.widths)):
        coefs = sum(exchange(plan, stage, [coefs] * (1 << plan.widths[stage])))
    for stage in range(1, len(plan.widths)):
        blocks = exchange(plan, stage, blocks)
        if stage + 1 < len(plan.widths):
            blocks = merge(plan, stage, inverse, blocks)
    return finish(plan, probes.shape[1], inverse, coefs, blocks)


def solution(mesh):
    return jax.shard_map(
        body,
        mesh=mesh,
        in_specs=(
            P(None, AXIS),
            P(AXIS),
            P(),
            P(AXIS, None, None),
            P(AXIS),
            P(AXIS),
            P(),
        ),
        out_specs=P(AXIS, None, None),
        check_vma=False,
    )
```

```python
import functools

import jax
import jax.numpy as jnp
from jax import lax
from jax.experimental import pallas as pl
from jax.experimental.pallas import tpu as pltpu
from jax.sharding import PartitionSpec as P

AXIS = "slab"
HIGHEST = lax.Precision.HIGHEST
LANES = 128
COEF_ROWS = 8
GROUP = 8
WIDE = 256
COEF_STEP = 4096
EARLY = 3
CHUNKS = 2


class Plan:
    def __init__(self, devices, tiles, entries, frames, block_width, tile_width):
        self.devices = devices
        self.tiles = tiles
        self.entries = entries
        self.frames = frames
        self.block_width = block_width
        self.tile_width = tile_width
        self.owned = tiles // devices
        self.log = devices.bit_length() - 1
        assert 1 << self.log == devices and self.owned * devices == tiles
        widths = [1]
        while sum(widths) < self.log:
            widths.append(min(2, self.log - sum(widths)))
        self.widths = widths
        self.done = [sum(widths[:i]) for i in range(len(widths) + 1)]
        self.slots = [
            min(self.owned, -(-(self.owned * (1 << b) + entries - 1) // devices))
            for b in self.done
        ]
        self.slots[-1] = self.owned
        self.owners = [devices >> self.done[i + 1] for i in range(len(widths))]

    def tiles_in(self, stage):
        return self.owners[stage] * self.slots[stage]

    def position(self, rel, stage):
        place = 0
        for i in range(stage, len(self.widths)):
            digit = (rel >> self.done[i]) & ((1 << self.widths[i]) - 1)
            place = (place << self.widths[i]) | digit
        return place

    def relative(self, place, stage):
        rel = 0
        for i in reversed(range(stage, len(self.widths))):
            rel = rel | ((place & ((1 << self.widths[i]) - 1)) << self.done[i])
            place = place >> self.widths[i]
        return rel


def tile_rows(index, frames):
    return pl.ds(pl.multiple_of(index * frames, 8), frames)


def split(values):
    high = values.astype(jnp.bfloat16)
    low = (values - high.astype(jnp.float32)).astype(jnp.bfloat16)
    return high, low


def demean(values):
    return values - jnp.sum(values, axis=0, keepdims=True) * (1.0 / values.shape[0])


def in_hbm(array):
    return pltpu.with_memory_space_constraint(array, pltpu.HBM)


def sample_kernel(
    plan, block_ids, tile_ids, tile_owner, series, weights,
    keep, send, picked, held, pick_sems, weight_sems,
):
    frames, width = plan.frames, plan.block_width
    groups = plan.entries // GROUP

    def pick(k):
        start = pl.multiple_of(block_ids[k] * width, width)
        return pltpu.make_async_copy(
            series.at[:, pl.ds(start, width)], picked.at[k], pick_sems.at[k]
        )

    def fetch(g):
        span = pl.ds(g * GROUP, GROUP)
        return pltpu.make_async_copy(weights.at[span], held.at[span], weight_sems.at[g])

    def begin(g, carry):
        fetch(g).start()
        for i in range(GROUP):
            pick(g * GROUP + i).start()
        return carry

    lax.fori_loop(0, groups, begin, 0)
    keep[...] = jnp.zeros_like(keep)
    send[...] = jnp.zeros_like(send)
    device = lax.axis_index(AXIS)
    spare = plan.owners[0] * plan.slots[0]

    def group(g, carry):
        fetch(g).wait()
        for i in range(GROUP):
            pick(g * GROUP + i).wait()
        for i in range(GROUP):
            k = g * GROUP + i
            tile = tile_ids[k]
            high, low = split(demean(picked[k]))
            both = jnp.dot(
                jnp.concatenate([high, low], axis=0),
                held[k],
                preferred_element_type=jnp.float32,
            )
            total = both[0:frames] + both[frames:]
            rel = tile_owner[tile & (plan.devices - 1)] ^ device
            offset = (tile - device * plan.owned) & (plan.tiles - 1)
            slot = plan.position(rel, 1) * plan.slots[0] + (offset >> plan.log)
            mine = (rel & 1) == 0
            used = tile >= 0
            to_keep = jnp.where(used & mine, slot, spare)
            to_send = jnp.where(used & jnp.logical_not(mine), slot, spare)
            keep[tile_rows(to_keep, frames), :] = total
            send[tile_rows(to_send, frames), :] = total
        return carry

    lax.fori_loop(0, groups, group, 0)


def sample(plan, series, weights, block_ids, tile_ids, tile_owner):
    frames, width = plan.frames, plan.block_width
    smem = pl.BlockSpec(memory_space=pltpu.SMEM)
    vmem = pl.BlockSpec(memory_space=pltpu.VMEM)
    hbm = pl.BlockSpec(memory_space=pl.ANY)
    block = jax.ShapeDtypeStruct(((plan.tiles_in(0) + 1) * frames, LANES), jnp.float32)
    held_bytes = plan.entries * width * (4 * frames + 2 * plan.tile_width)
    return pl.pallas_call(
        functools.partial(sample_kernel, plan),
        name="sample",
        in_specs=[smem, smem, smem, hbm, hbm],
        out_specs=[vmem, vmem],
        out_shape=[block, block],
        scratch_shapes=[
            pltpu.VMEM((plan.entries, frames, width), jnp.float32),
            pltpu.VMEM(weights.shape, weights.dtype),
            pltpu.SemaphoreType.DMA((plan.entries,)),
            pltpu.SemaphoreType.DMA((plan.entries // GROUP,)),
        ],
        compiler_params=pltpu.CompilerParams(
            vmem_limit_bytes=held_bytes + 8 * block.shape[0] * LANES + (6 << 20)
        ),
    )(*[in_hbm(x) for x in (block_ids, tile_ids, tile_owner, series, weights)])


def coef_kernel(
    first, steps, series, mask, probes, before, coefs,
    held, marks, halves, masked, gram, sems, mark_sem,
):
    frames = series.shape[0]
    columns = COEF_STEP

    def fetch(step):
        span = pl.ds(pl.multiple_of(step * columns, columns), columns)
        there = pl.ds(pl.multiple_of((first + step) * columns, columns), columns)
        return pltpu.make_async_copy(series.at[:, there], held.at[:, span], sems.at[step])

    mark_copy = pltpu.make_async_copy(
        mask.at[:, pl.ds(first * columns, steps * columns)], marks, mark_sem
    )
    mark_copy.start()
    for step in range(steps):
        fetch(step).start()
    gram[...] = jnp.zeros_like(gram)
    mark_copy.wait()

    def chunk(step, carry):
        fetch(step).wait()
        start = step * columns
        for at in range(0, columns, WIDE):
            span = pl.ds(pl.multiple_of(start + at, WIDE), WIDE)
            place = pl.ds(at, WIDE)
            high, low = split(demean(held[:, span]))
            halves[0:frames, place] = high
            halves[frames:, place] = low
            masked[:, place] = high * marks[:, span].astype(jnp.float32).astype(jnp.bfloat16)
        gram[...] += lax.dot_general(
            halves[...],
            masked[...],
            (((1,), (1,)), ((), ())),
            preferred_element_type=jnp.float32,
        )
        return carry

    lax.fori_loop(0, steps, chunk, 0)
    low = gram[frames:, :]
    start = probes[...]
    made = jnp.dot(
        start, gram[0:frames, :] + low, precision=HIGHEST, preferred_element_type=jnp.float32
    ) + lax.dot_general(
        start,
        low,
        (((1,), (1,)), ((), ())),
        precision=HIGHEST,
        preferred_element_type=jnp.float32,
    )
    coefs[...] = before[...]
    coefs[0 : start.shape[0], 0:frames] += made


def local_coefs(series, noise_mask, probes, before, first, steps):
    frames, voxels = series.shape
    held = steps * COEF_STEP
    vmem = pl.BlockSpec(memory_space=pltpu.VMEM)
    hbm = pl.BlockSpec(memory_space=pl.ANY)
    return pl.pallas_call(
        functools.partial(coef_kernel, first, steps),
        name="coefs",
        in_specs=[hbm, hbm, vmem, vmem],
        out_specs=vmem,
        out_shape=jax.ShapeDtypeStruct(before.shape, before.dtype),
        scratch_shapes=[
            pltpu.VMEM((frames, held), series.dtype),
            pltpu.VMEM((1, held), noise_mask.dtype),
            pltpu.VMEM((2 * frames, COEF_STEP), jnp.bfloat16),
            pltpu.VMEM((frames, COEF_STEP), jnp.bfloat16),
            pltpu.VMEM((2 * frames, frames), jnp.float32),
            pltpu.SemaphoreType.DMA((steps,)),
            pltpu.SemaphoreType.DMA,
        ],
        compiler_params=pltpu.CompilerParams(vmem_limit_bytes=24 << 20),
        cost_estimate=pl.CostEstimate(
            flops=4 * frames * frames * held,
            bytes_accessed=4 * frames * held,
            transcendentals=0,
        ),
    )(in_hbm(series), in_hbm(noise_mask.reshape(1, voxels)), probes.T, before)


def note_owners(plan, tile_owner, inverse):
    for residue in range(plan.devices):
        inverse[tile_owner[residue]] = residue


def add_tiles(plan, stage, inverse, sources, place, slot, height, skip=0, rows=None):
    rows = height if rows is None else rows
    device = lax.axis_index(AXIS)
    done, after = plan.done[stage], plan.done[stage + 1]
    slots, devices, tiles = plan.slots[stage], plan.devices, plan.tiles
    residue = inverse[device ^ plan.relative(place, stage + 1)]
    last = stage + 1 == len(plan.widths)
    base = 0 if last else ((device >> after) << after) * plan.owned
    tile = (base + ((residue - base) & (devices - 1)) + slot * devices) & (tiles - 1)
    total = None
    for digit, source in enumerate(sources):
        sender = device ^ (digit << done)
        first = ((sender >> done) << done) * plan.owned
        offset = (tile - first) & (tiles - 1)
        there = offset < slots * devices
        at = place * slots + jnp.minimum(offset >> plan.log, slots - 1)
        value = source[pl.ds(pl.multiple_of(at * height + skip, 8), rows), :]
        value = jnp.where(there, value, 0.0)
        total = value if total is None else total + value
    return total


def add_coefs(sources):
    total = None
    for source in sources:
        value = source[pl.ds(source.shape[0] - COEF_ROWS, COEF_ROWS), :]
        total = value if total is None else total + value
    return total


def merge_kernel(plan, stage, span, fresh, tile_owner, *refs):
    fan = 1 << plan.widths[stage]
    sources, refs = refs[:fan], refs[fan:]
    coefs = None
    if fresh:
        coefs, refs = refs[0][...] + refs[1][...], refs[2:]
    outs, inverse = refs[:-1], refs[-1]
    begin, rows = span
    slots, count = plan.slots[stage + 1], plan.owners[stage + 1]
    size = count * slots * rows
    note_owners(plan, tile_owner, inverse)
    if outs[0].shape[0] > size:
        if not fresh:
            coefs = add_coefs(sources)
        for out in outs:
            out[pl.ds(size, COEF_ROWS), :] = coefs
    height, skip = (plan.frames, begin) if stage == 0 else (rows, 0)
    for digit, out in enumerate(outs):

        def owner(rest, carry):
            for slot in range(slots):
                value = add_tiles(
                    plan, stage, inverse, sources, digit * count + rest, slot,
                    height, skip, rows,
                )
                target = pl.ds(pl.multiple_of((rest * slots + slot) * rows, 8), rows)
                out[target, :] = value
            return carry

        if count <= 4:
            for rest in range(count):
                owner(rest, 0)
        else:
            lax.fori_loop(0, count, owner, 0)


def merge(plan, stage, span, riding, tile_owner, sources, coefs=()):
    fan = 1 << plan.widths[stage + 1]
    rows = plan.tiles_in(stage + 1) * span[1] + (COEF_ROWS if riding else 0)
    block = jax.ShapeDtypeStruct((rows, LANES), jnp.float32)
    vmem = pl.BlockSpec(memory_space=pltpu.VMEM)
    arrays = list(sources) + list(coefs)
    return pl.pallas_call(
        functools.partial(merge_kernel, plan, stage, span, len(coefs) > 0),
        name="merge",
        in_specs=[pl.BlockSpec(memory_space=pltpu.SMEM)] + [vmem] * len(arrays),
        out_specs=[vmem] * fan,
        out_shape=[block] * fan,
        scratch_shapes=[pltpu.SMEM((plan.devices,), jnp.int32)],
        compiler_params=pltpu.CompilerParams(vmem_limit_bytes=32 << 20),
    )(in_hbm(tile_owner), *arrays)


def finish_kernel(plan, comps, spans, tile_owner, *refs):
    stage = len(plan.widths) - 1
    fan = 1 << plan.widths[stage]
    parts = [refs[i * fan : (i + 1) * fan] for i in range(len(spans))]
    out, inverse = refs[-2:]
    frames = plan.frames
    note_owners(plan, tile_owner, inverse)
    basis = add_coefs(parts[-1])
    lane = lax.broadcasted_iota(jnp.int32, basis.shape, 1)
    row = lax.broadcasted_iota(jnp.int32, basis.shape, 0)
    basis = jnp.where((lane < frames) & (row < comps), basis, 0.0)
    unit = jnp.zeros_like(basis)
    for i in range(comps):
        line = basis[i : i + 1, :]
        line = line * lax.rsqrt(jnp.sum(line * line, axis=1, keepdims=True))
        unit = jnp.where(row == i, line, unit)
        basis = basis - jnp.sum(basis * line, axis=1, keepdims=True) * line
    unit = unit[:, 0:frames]
    values = []
    for slot in range(plan.owned):
        pieces = [
            add_tiles(plan, stage, inverse, sources, 0, slot, rows)
            for (begin, rows), sources in zip(spans, parts)
        ]
        values.append(jnp.concatenate(pieces, axis=0))
    value = jnp.concatenate(values, axis=1)
    along = jnp.dot(unit, value, precision=HIGHEST, preferred_element_type=jnp.float32)
    value = value - lax.dot_general(
        unit,
        along,
        (((0,), (0,)), ((), ())),
        precision=HIGHEST,
        preferred_element_type=jnp.float32,
    )
    for slot in range(plan.owned):
        out[slot] = value[:, slot * plan.tile_width : (slot + 1) * plan.tile_width]


def finish(plan, comps, spans, tile_owner, parts):
    vmem = pl.BlockSpec(memory_space=pltpu.VMEM)
    arrays = [block for part in parts for block in part]
    return pl.pallas_call(
        functools.partial(finish_kernel, plan, comps, spans),
        name="finish",
        in_specs=[pl.BlockSpec(memory_space=pltpu.SMEM)] + [vmem] * len(arrays),
        out_specs=vmem,
        out_shape=jax.ShapeDtypeStruct((plan.owned, plan.frames, plan.tile_width), jnp.float32),
        scratch_shapes=[pltpu.SMEM((plan.devices,), jnp.int32)],
        compiler_params=pltpu.CompilerParams(vmem_limit_bytes=32 << 20),
    )(in_hbm(tile_owner), *arrays)


def exchange(plan, stage, blocks):
    received = [blocks[0]]
    for digit in range(1, len(blocks)):
        pairs = [(i, i ^ (digit << plan.done[stage])) for i in range(plan.devices)]
        received.append(lax.ppermute(blocks[digit], AXIS, pairs))
    return received


def body(series, noise_mask, probes, sample_weights, block_ids, tile_ids, tile_owner):
    frames, voxels = series.shape
    entries, block_width, tile_width = sample_weights.shape
    plan = Plan(
        lax.axis_size(AXIS), tile_owner.shape[0], entries, frames, block_width, tile_width
    )
    stages = len(plan.widths)
    rows = frames // CHUNKS
    spans = [(i * rows, rows) for i in range(CHUNKS)]
    steps = voxels // COEF_STEP
    keep, send = sample(plan, series, sample_weights, block_ids, tile_ids, tile_owner)
    keep, send, probes = lax.optimization_barrier((keep, send, probes))
    pair = exchange(plan, 0, [keep, send])
    coefs = jnp.zeros((COEF_ROWS, LANES), jnp.float32)
    coefs = local_coefs(series, noise_mask, probes, coefs, 0, EARLY)
    chunks = [merge(plan, 0, span, False, tile_owner, pair) for span in spans[:-1]]
    chunks[-1], coefs = lax.optimization_barrier((chunks[-1], coefs))
    coefs = local_coefs(series, noise_mask, probes, coefs, EARLY, steps - EARLY)
    coefs = exchange(plan, 0, [coefs, coefs])
    chunks.append(merge(plan, 0, spans[-1], True, tile_owner, pair, coefs))
    for stage in range(1, stages):
        for i, span in enumerate(spans):
            chunks[i] = exchange(plan, stage, chunks[i])
            if stage + 1 < stages:
                riding = i + 1 == len(spans)
                chunks[i] = merge(plan, stage, span, riding, tile_owner, chunks[i])
    return finish(plan, probes.shape[1], spans, tile_owner, chunks)


def solution(mesh):
    return jax.shard_map(
        body,
        mesh=mesh,
        in_specs=(
            P(None, AXIS),
            P(AXIS),
            P(),
            P(AXIS, None, None),
            P(AXIS),
            P(AXIS),
            P(),
        ),
        out_specs=P(AXIS, None, None),
        check_vma=False,
    )
```

```python
import functools

import jax
import jax.numpy as jnp
from jax import lax
from jax.experimental import pallas as pl
from jax.experimental.pallas import tpu as pltpu
from jax.sharding import PartitionSpec as P

AXIS = "slab"
HIGHEST = lax.Precision.HIGHEST
LANES = 128
COEF_ROWS = 8
GROUP = 8
WIDE = 256
COEF_STEP = 4096
EARLY = 3
CHUNKS = 2


class Plan:
    def __init__(self, devices, tiles, entries, frames, block_width, tile_width):
        self.devices = devices
        self.tiles = tiles
        self.entries = entries
        self.frames = frames
        self.block_width = block_width
        self.tile_width = tile_width
        self.owned = tiles // devices
        self.log = devices.bit_length() - 1
        assert 1 << self.log == devices and self.owned * devices == tiles
        widths = [1]
        while sum(widths) < self.log:
            widths.append(min(2, self.log - sum(widths)))
        self.widths = widths
        self.done = [sum(widths[:i]) for i in range(len(widths) + 1)]
        self.slots = [
            min(self.owned, -(-(self.owned * (1 << b) + entries - 1) // devices))
            for b in self.done
        ]
        self.slots[-1] = self.owned
        self.owners = [devices >> self.done[i + 1] for i in range(len(widths))]

    def tiles_in(self, stage):
        return self.owners[stage] * self.slots[stage]

    def position(self, rel, stage):
        place = 0
        for i in range(stage, len(self.widths)):
            digit = (rel >> self.done[i]) & ((1 << self.widths[i]) - 1)
            place = (place << self.widths[i]) | digit
        return place

    def relative(self, place, stage):
        rel = 0
        for i in reversed(range(stage, len(self.widths))):
            rel = rel | ((place & ((1 << self.widths[i]) - 1)) << self.done[i])
            place = place >> self.widths[i]
        return rel


def tile_rows(index, frames):
    return pl.ds(pl.multiple_of(index * frames, 8), frames)


def split(values):
    high = values.astype(jnp.bfloat16)
    low = (values - high.astype(jnp.float32)).astype(jnp.bfloat16)
    return high, low


def demean(values):
    return values - jnp.sum(values, axis=0, keepdims=True) * (1.0 / values.shape[0])


def in_hbm(array):
    return pltpu.with_memory_space_constraint(array, pltpu.HBM)


def sample_kernel(
    plan, block_ids, tile_ids, tile_owner, series, weights,
    keep, send, picked, held, pick_sems, weight_sems,
):
    frames, width = plan.frames, plan.block_width
    groups = plan.entries // GROUP

    def pick(k):
        start = pl.multiple_of(block_ids[k] * width, width)
        return pltpu.make_async_copy(
            series.at[:, pl.ds(start, width)], picked.at[k], pick_sems.at[k]
        )

    def fetch(g):
        span = pl.ds(g * GROUP, GROUP)
        return pltpu.make_async_copy(weights.at[span], held.at[span], weight_sems.at[g])

    def begin(g, carry):
        fetch(g).start()
        for i in range(GROUP):
            pick(g * GROUP + i).start()
        return carry

    lax.fori_loop(0, groups, begin, 0)
    keep[...] = jnp.zeros_like(keep)
    send[...] = jnp.zeros_like(send)
    device = lax.axis_index(AXIS)
    spare = plan.owners[0] * plan.slots[0]

    def group(g, carry):
        fetch(g).wait()
        for i in range(GROUP):
            pick(g * GROUP + i).wait()
        for i in range(GROUP):
            k = g * GROUP + i
            tile = tile_ids[k]
            high, low = split(demean(picked[k]))
            both = jnp.dot(
                jnp.concatenate([high, low], axis=0),
                held[k],
                preferred_element_type=jnp.float32,
            )
            total = both[0:frames] + both[frames:]
            rel = tile_owner[tile & (plan.devices - 1)] ^ device
            offset = (tile - device * plan.owned) & (plan.tiles - 1)
            slot = plan.position(rel, 1) * plan.slots[0] + (offset >> plan.log)
            mine = (rel & 1) == 0
            used = tile >= 0
            to_keep = jnp.where(used & mine, slot, spare)
            to_send = jnp.where(used & jnp.logical_not(mine), slot, spare)
            keep[tile_rows(to_keep, frames), :] = total
            send[tile_rows(to_send, frames), :] = total
        return carry

    lax.fori_loop(0, groups, group, 0)


def sample(plan, series, weights, block_ids, tile_ids, tile_owner):
    frames, width = plan.frames, plan.block_width
    smem = pl.BlockSpec(memory_space=pltpu.SMEM)
    vmem = pl.BlockSpec(memory_space=pltpu.VMEM)
    hbm = pl.BlockSpec(memory_space=pl.ANY)
    block = jax.ShapeDtypeStruct(((plan.tiles_in(0) + 1) * frames, LANES), jnp.float32)
    held_bytes = plan.entries * width * (4 * frames + 2 * plan.tile_width)
    return pl.pallas_call(
        functools.partial(sample_kernel, plan),
        name="sample",
        in_specs=[smem, smem, smem, hbm, hbm],
        out_specs=[vmem, vmem],
        out_shape=[block, block],
        scratch_shapes=[
            pltpu.VMEM((plan.entries, frames, width), jnp.float32),
            pltpu.VMEM(weights.shape, weights.dtype),
            pltpu.SemaphoreType.DMA((plan.entries,)),
            pltpu.SemaphoreType.DMA((plan.entries // GROUP,)),
        ],
        compiler_params=pltpu.CompilerParams(
            vmem_limit_bytes=held_bytes + 8 * block.shape[0] * LANES + (6 << 20)
        ),
    )(*[in_hbm(x) for x in (block_ids, tile_ids, tile_owner, series, weights)])


def coef_kernel(
    first, steps, series, mask, probes, before, coefs,
    held, marks, halves, masked, gram, sems, mark_sem,
):
    frames = series.shape[0]
    columns = COEF_STEP

    def fetch(step):
        span = pl.ds(pl.multiple_of(step * columns, columns), columns)
        there = pl.ds(pl.multiple_of((first + step) * columns, columns), columns)
        return pltpu.make_async_copy(series.at[:, there], held.at[:, span], sems.at[step])

    mark_copy = pltpu.make_async_copy(
        mask.at[:, pl.ds(first * columns, steps * columns)], marks, mark_sem
    )
    mark_copy.start()
    for step in range(steps):
        fetch(step).start()
    gram[...] = jnp.zeros_like(gram)
    mark_copy.wait()

    def chunk(step, carry):
        fetch(step).wait()
        start = step * columns
        for at in range(0, columns, WIDE):
            span = pl.ds(pl.multiple_of(start + at, WIDE), WIDE)
            place = pl.ds(at, WIDE)
            high, low = split(demean(held[:, span]))
            halves[0:frames, place] = high
            halves[frames:, place] = low
            masked[:, place] = high * marks[:, span].astype(jnp.float32).astype(jnp.bfloat16)
        gram[...] += lax.dot_general(
            halves[...],
            masked[...],
            (((1,), (1,)), ((), ())),
            preferred_element_type=jnp.float32,
        )
        return carry

    lax.fori_loop(0, steps, chunk, 0)
    low = gram[frames:, :]
    start = probes[...]
    made = jnp.dot(
        start, gram[0:frames, :] + low, precision=HIGHEST, preferred_element_type=jnp.float32
    ) + lax.dot_general(
        start,
        low,
        (((1,), (1,)), ((), ())),
        precision=HIGHEST,
        preferred_element_type=jnp.float32,
    )
    coefs[...] = before[...]
    coefs[0 : start.shape[0], 0:frames] += made


def local_coefs(series, noise_mask, probes, before, first, steps):
    frames, voxels = series.shape
    held = steps * COEF_STEP
    vmem = pl.BlockSpec(memory_space=pltpu.VMEM)
    hbm = pl.BlockSpec(memory_space=pl.ANY)
    return pl.pallas_call(
        functools.partial(coef_kernel, first, steps),
        name="coefs",
        in_specs=[hbm, hbm, vmem, vmem],
        out_specs=vmem,
        out_shape=jax.ShapeDtypeStruct(before.shape, before.dtype),
        scratch_shapes=[
            pltpu.VMEM((frames, held), series.dtype),
            pltpu.VMEM((1, held), noise_mask.dtype),
            pltpu.VMEM((2 * frames, COEF_STEP), jnp.bfloat16),
            pltpu.VMEM((frames, COEF_STEP), jnp.bfloat16),
            pltpu.VMEM((2 * frames, frames), jnp.float32),
            pltpu.SemaphoreType.DMA((steps,)),
            pltpu.SemaphoreType.DMA,
        ],
        compiler_params=pltpu.CompilerParams(vmem_limit_bytes=24 << 20),
        cost_estimate=pl.CostEstimate(
            flops=4 * frames * frames * held,
            bytes_accessed=4 * frames * held,
            transcendentals=0,
        ),
    )(in_hbm(series), in_hbm(noise_mask.reshape(1, voxels)), probes.T, before)


def note_owners(plan, tile_owner, inverse):
    for residue in range(plan.devices):
        inverse[tile_owner[residue]] = residue


def add_tiles(plan, stage, inverse, sources, place, slot, height, skip=0, rows=None):
    rows = height if rows is None else rows
    device = lax.axis_index(AXIS)
    done, after = plan.done[stage], plan.done[stage + 1]
    slots, devices, tiles = plan.slots[stage], plan.devices, plan.tiles
    residue = inverse[device ^ plan.relative(place, stage + 1)]
    last = stage + 1 == len(plan.widths)
    base = 0 if last else ((device >> after) << after) * plan.owned
    tile = (base + ((residue - base) & (devices - 1)) + slot * devices) & (tiles - 1)
    total = None
    for digit, source in enumerate(sources):
        sender = device ^ (digit << done)
        first = ((sender >> done) << done) * plan.owned
        offset = (tile - first) & (tiles - 1)
        there = offset < slots * devices
        at = place * slots + jnp.minimum(offset >> plan.log, slots - 1)
        value = source[pl.ds(pl.multiple_of(at * height + skip, 8), rows), :]
        value = jnp.where(there, value, 0.0)
        total = value if total is None else total + value
    return total


def add_coefs(sources):
    total = None
    for source in sources:
        value = source[pl.ds(source.shape[0] - COEF_ROWS, COEF_ROWS), :]
        total = value if total is None else total + value
    return total


def merge_kernel(plan, stage, span, fresh, tile_owner, *refs):
    fan = 1 << plan.widths[stage]
    sources, refs = refs[:fan], refs[fan:]
    coefs = None
    if fresh:
        coefs, refs = refs[0][...] + refs[1][...], refs[2:]
    outs, inverse = refs[:-1], refs[-1]
    begin, rows = span
    slots, count = plan.slots[stage + 1], plan.owners[stage + 1]
    size = count * slots * rows
    note_owners(plan, tile_owner, inverse)
    if outs[0].shape[0] > size:
        if not fresh:
            coefs = add_coefs(sources)
        for out in outs:
            out[pl.ds(size, COEF_ROWS), :] = coefs
    height, skip = (plan.frames, begin) if stage == 0 else (rows, 0)
    for digit, out in enumerate(outs):

        def owner(rest, carry):
            for slot in range(slots):
                value = add_tiles(
                    plan, stage, inverse, sources, digit * count + rest, slot,
                    height, skip, rows,
                )
                target = pl.ds(pl.multiple_of((rest * slots + slot) * rows, 8), rows)
                out[target, :] = value
            return carry

        if count <= 4:
            for rest in range(count):
                owner(rest, 0)
        else:
            lax.fori_loop(0, count, owner, 0)


def merge(plan, stage, span, riding, tile_owner, sources, coefs=()):
    fan = 1 << plan.widths[stage + 1]
    rows = plan.tiles_in(stage + 1) * span[1] + (COEF_ROWS if riding else 0)
    block = jax.ShapeDtypeStruct((rows, LANES), jnp.float32)
    vmem = pl.BlockSpec(memory_space=pltpu.VMEM)
    arrays = list(sources) + list(coefs)
    return pl.pallas_call(
        functools.partial(merge_kernel, plan, stage, span, len(coefs) > 0),
        name="merge",
        in_specs=[pl.BlockSpec(memory_space=pltpu.SMEM)] + [vmem] * len(arrays),
        out_specs=[vmem] * fan,
        out_shape=[block] * fan,
        scratch_shapes=[pltpu.SMEM((plan.devices,), jnp.int32)],
        compiler_params=pltpu.CompilerParams(vmem_limit_bytes=32 << 20),
    )(in_hbm(tile_owner), *arrays)


def finish_kernel(plan, comps, spans, tile_owner, *refs):
    stage = len(plan.widths) - 1
    fan = 1 << plan.widths[stage]
    parts = [refs[i * fan : (i + 1) * fan] for i in range(len(spans))]
    out, inverse = refs[-2:]
    frames = plan.frames
    note_owners(plan, tile_owner, inverse)
    basis = add_coefs(parts[-1])
    lane = lax.broadcasted_iota(jnp.int32, basis.shape, 1)
    row = lax.broadcasted_iota(jnp.int32, basis.shape, 0)
    basis = jnp.where((lane < frames) & (row < comps), basis, 0.0)
    unit = jnp.zeros_like(basis)
    for i in range(comps):
        line = basis[i : i + 1, :]
        line = line * lax.rsqrt(jnp.sum(line * line, axis=1, keepdims=True))
        unit = jnp.where(row == i, line, unit)
        basis = basis - jnp.sum(basis * line, axis=1, keepdims=True) * line
    unit = unit[:, 0:frames]
    values = []
    for slot in range(plan.owned):
        pieces = [
            add_tiles(plan, stage, inverse, sources, 0, slot, rows)
            for (begin, rows), sources in zip(spans, parts)
        ]
        values.append(jnp.concatenate(pieces, axis=0))
    value = jnp.concatenate(values, axis=1)
    along = jnp.dot(unit, value, precision=HIGHEST, preferred_element_type=jnp.float32)
    value = value - lax.dot_general(
        unit,
        along,
        (((0,), (0,)), ((), ())),
        precision=HIGHEST,
        preferred_element_type=jnp.float32,
    )
    for slot in range(plan.owned):
        out[slot] = value[:, slot * plan.tile_width : (slot + 1) * plan.tile_width]


def finish(plan, comps, spans, tile_owner, parts):
    vmem = pl.BlockSpec(memory_space=pltpu.VMEM)
    arrays = [block for part in parts for block in part]
    return pl.pallas_call(
        functools.partial(finish_kernel, plan, comps, spans),
        name="finish",
        in_specs=[pl.BlockSpec(memory_space=pltpu.SMEM)] + [vmem] * len(arrays),
        out_specs=vmem,
        out_shape=jax.ShapeDtypeStruct((plan.owned, plan.frames, plan.tile_width), jnp.float32),
        scratch_shapes=[pltpu.SMEM((plan.devices,), jnp.int32)],
        compiler_params=pltpu.CompilerParams(vmem_limit_bytes=32 << 20),
    )(in_hbm(tile_owner), *arrays)


def exchange(plan, stage, blocks):
    received = [blocks[0]]
    for digit in range(1, len(blocks)):
        pairs = [(i, i ^ (digit << plan.done[stage])) for i in range(plan.devices)]
        received.append(lax.ppermute(blocks[digit], AXIS, pairs))
    return received


def body(series, noise_mask, probes, sample_weights, block_ids, tile_ids, tile_owner):
    frames, voxels = series.shape
    entries, block_width, tile_width = sample_weights.shape
    plan = Plan(
        lax.axis_size(AXIS), tile_owner.shape[0], entries, frames, block_width, tile_width
    )
    stages = len(plan.widths)
    rows = frames // CHUNKS
    spans = [(i * rows, rows) for i in range(CHUNKS)]
    steps = voxels // COEF_STEP
    keep, send = sample(plan, series, sample_weights, block_ids, tile_ids, tile_owner)
    keep, send, probes = lax.optimization_barrier((keep, send, probes))
    pair = exchange(plan, 0, [keep, send])
    coefs = jnp.zeros((COEF_ROWS, LANES), jnp.float32)
    coefs = local_coefs(series, noise_mask, probes, coefs, 0, EARLY)
    chunks = [merge(plan, 0, span, False, tile_owner, pair) for span in spans[:-1]]
    chunks[-1], coefs = lax.optimization_barrier((chunks[-1], coefs))
    coefs = local_coefs(series, noise_mask, probes, coefs, EARLY, steps - EARLY)
    coefs = exchange(plan, 0, [coefs, coefs])
    chunks.append(merge(plan, 0, spans[-1], True, tile_owner, pair, coefs))
    for stage in range(1, stages):
        for i, span in enumerate(spans):
            if stage + 1 == stages and i > 0:
                far, chunks[i] = lax.optimization_barrier((chunks[i - 1][2:], chunks[i]))
                chunks[i - 1] = chunks[i - 1][:2] + far
            chunks[i] = exchange(plan, stage, chunks[i])
            if stage + 1 < stages:
                riding = i + 1 == len(spans)
                chunks[i] = merge(plan, stage, span, riding, tile_owner, chunks[i])
    return finish(plan, probes.shape[1], spans, tile_owner, chunks)


def solution(mesh):
    return jax.shard_map(
        body,
        mesh=mesh,
        in_specs=(
            P(None, AXIS),
            P(AXIS),
            P(),
            P(AXIS, None, None),
            P(AXIS),
            P(AXIS),
            P(),
        ),
        out_specs=P(AXIS, None, None),
        check_vma=False,
    )
```

```python
import functools

import jax
import jax.numpy as jnp
from jax import lax
from jax.experimental import pallas as pl
from jax.experimental.pallas import tpu as pltpu
from jax.sharding import PartitionSpec as P

AXIS = "slab"
HIGHEST = lax.Precision.HIGHEST
LANES = 128
COEF_ROWS = 8
GROUP = 16
AHEAD = 3
WIDE = 256
COEF_STEP = 4096
EARLY = 3
CHUNKS = 2


class Plan:
    def __init__(self, devices, tiles, entries, frames, block_width, tile_width):
        self.devices = devices
        self.tiles = tiles
        self.entries = entries
        self.frames = frames
        self.block_width = block_width
        self.tile_width = tile_width
        self.owned = tiles // devices
        self.log = devices.bit_length() - 1
        assert 1 << self.log == devices and self.owned * devices == tiles
        widths = [1]
        while sum(widths) < self.log:
            widths.append(min(2, self.log - sum(widths)))
        self.widths = widths
        self.done = [sum(widths[:i]) for i in range(len(widths) + 1)]
        self.slots = [
            min(self.owned, -(-(self.owned * (1 << b) + entries - 1) // devices))
            for b in self.done
        ]
        self.slots[-1] = self.owned
        self.owners = [devices >> self.done[i + 1] for i in range(len(widths))]

    def tiles_in(self, stage):
        return self.owners[stage] * self.slots[stage]

    def position(self, rel, stage):
        place = 0
        for i in range(stage, len(self.widths)):
            digit = (rel >> self.done[i]) & ((1 << self.widths[i]) - 1)
            place = (place << self.widths[i]) | digit
        return place

    def relative(self, place, stage):
        rel = 0
        for i in reversed(range(stage, len(self.widths))):
            rel = rel | ((place & ((1 << self.widths[i]) - 1)) << self.done[i])
            place = place >> self.widths[i]
        return rel


def tile_rows(index, frames):
    return pl.ds(pl.multiple_of(index * frames, 8), frames)


def split(values):
    high = values.astype(jnp.bfloat16)
    low = (values - high.astype(jnp.float32)).astype(jnp.bfloat16)
    return high, low


def demean(values):
    return values - jnp.sum(values, axis=0, keepdims=True) * (1.0 / values.shape[0])


def in_hbm(array):
    return pltpu.with_memory_space_constraint(array, pltpu.HBM)


def sample_kernel(
    plan, block_ids, tile_ids, tile_owner, series, weights,
    keep, send, picked, held, pick_sems, weight_sems,
):
    frames, width = plan.frames, plan.block_width
    groups = plan.entries // GROUP

    def pick(k):
        start = pl.multiple_of(block_ids[k] * width, width)
        return pltpu.make_async_copy(
            series.at[:, pl.ds(start, width)], picked.at[k], pick_sems.at[k]
        )

    def fetch(g):
        span = pl.ds(g * GROUP, GROUP)
        return pltpu.make_async_copy(weights.at[span], held.at[span], weight_sems.at[g])

    def begin(g, carry):
        fetch(g).start()
        for i in range(GROUP):
            pick(g * GROUP + i).start()
        return carry

    lax.fori_loop(0, groups, begin, 0)
    keep[...] = jnp.zeros_like(keep)
    send[...] = jnp.zeros_like(send)
    device = lax.axis_index(AXIS)
    spare = plan.owners[0] * plan.slots[0]

    def group(g, carry):
        fetch(g).wait()
        for i in range(GROUP):
            pick(g * GROUP + i).wait()
        for i in range(GROUP):
            k = g * GROUP + i
            tile = tile_ids[k]
            high, low = split(demean(picked[k]))
            both = jnp.dot(
                jnp.concatenate([high, low], axis=0),
                held[k],
                preferred_element_type=jnp.float32,
            )
            total = both[0:frames] + both[frames:]
            rel = tile_owner[tile & (plan.devices - 1)] ^ device
            offset = (tile - device * plan.owned) & (plan.tiles - 1)
            slot = plan.position(rel, 1) * plan.slots[0] + (offset >> plan.log)
            mine = (rel & 1) == 0
            used = tile >= 0
            to_keep = jnp.where(used & mine, slot, spare)
            to_send = jnp.where(used & jnp.logical_not(mine), slot, spare)
            keep[tile_rows(to_keep, frames), :] = total
            send[tile_rows(to_send, frames), :] = total
        return carry

    lax.fori_loop(0, groups, group, 0)


def sample(plan, series, weights, block_ids, tile_ids, tile_owner):
    frames, width = plan.frames, plan.block_width
    smem = pl.BlockSpec(memory_space=pltpu.SMEM)
    vmem = pl.BlockSpec(memory_space=pltpu.VMEM)
    hbm = pl.BlockSpec(memory_space=pl.ANY)
    block = jax.ShapeDtypeStruct(((plan.tiles_in(0) + 1) * frames, LANES), jnp.float32)
    held_bytes = plan.entries * width * (4 * frames + 2 * plan.tile_width)
    return pl.pallas_call(
        functools.partial(sample_kernel, plan),
        name="sample",
        in_specs=[smem, smem, smem, hbm, hbm],
        out_specs=[vmem, vmem],
        out_shape=[block, block],
        scratch_shapes=[
            pltpu.VMEM((plan.entries, frames, width), jnp.float32),
            pltpu.VMEM(weights.shape, weights.dtype),
            pltpu.SemaphoreType.DMA((plan.entries,)),
            pltpu.SemaphoreType.DMA((plan.entries // GROUP,)),
        ],
        compiler_params=pltpu.CompilerParams(
            vmem_limit_bytes=held_bytes + 8 * block.shape[0] * LANES + (6 << 20)
        ),
    )(*[in_hbm(x) for x in (block_ids, tile_ids, tile_owner, series, weights)])


def coef_kernel(
    first, steps, series, mask, probes, before, coefs,
    held, marks, halves, masked, gram, sems, mark_sem,
):
    frames = series.shape[0]
    columns = COEF_STEP

    def fetch(step):
        span = pl.ds(pl.multiple_of(step * columns, columns), columns)
        there = pl.ds(pl.multiple_of((first + step) * columns, columns), columns)
        return pltpu.make_async_copy(series.at[:, there], held.at[:, span], sems.at[step])

    mark_copy = pltpu.make_async_copy(
        mask.at[:, pl.ds(first * columns, steps * columns)], marks, mark_sem
    )
    mark_copy.start()
    for step in range(min(AHEAD, steps)):
        fetch(step).start()
    gram[...] = jnp.zeros_like(gram)
    mark_copy.wait()

    def chunk(step, carry):
        fetch(step).wait()

        @pl.when(step + AHEAD < steps)
        def _():
            fetch(step + AHEAD).start()

        start = step * columns
        for at in range(0, columns, WIDE):
            span = pl.ds(pl.multiple_of(start + at, WIDE), WIDE)
            place = pl.ds(at, WIDE)
            high, low = split(demean(held[:, span]))
            halves[0:frames, place] = high
            halves[frames:, place] = low
            masked[:, place] = high * marks[:, span].astype(jnp.float32).astype(jnp.bfloat16)
        gram[...] += lax.dot_general(
            halves[...],
            masked[...],
            (((1,), (1,)), ((), ())),
            preferred_element_type=jnp.float32,
        )
        return carry

    lax.fori_loop(0, steps, chunk, 0)
    low = gram[frames:, :]
    start = probes[...]
    made = jnp.dot(
        start, gram[0:frames, :] + low, precision=HIGHEST, preferred_element_type=jnp.float32
    ) + lax.dot_general(
        start,
        low,
        (((1,), (1,)), ((), ())),
        precision=HIGHEST,
        preferred_element_type=jnp.float32,
    )
    coefs[...] = before[...]
    coefs[0 : start.shape[0], 0:frames] += made


def local_coefs(series, noise_mask, probes, before, first, steps):
    frames, voxels = series.shape
    held = steps * COEF_STEP
    vmem = pl.BlockSpec(memory_space=pltpu.VMEM)
    hbm = pl.BlockSpec(memory_space=pl.ANY)
    return pl.pallas_call(
        functools.partial(coef_kernel, first, steps),
        name="coefs",
        in_specs=[hbm, hbm, vmem, vmem],
        out_specs=vmem,
        out_shape=jax.ShapeDtypeStruct(before.shape, before.dtype),
        scratch_shapes=[
            pltpu.VMEM((frames, held), series.dtype),
            pltpu.VMEM((1, held), noise_mask.dtype),
            pltpu.VMEM((2 * frames, COEF_STEP), jnp.bfloat16),
            pltpu.VMEM((frames, COEF_STEP), jnp.bfloat16),
            pltpu.VMEM((2 * frames, frames), jnp.float32),
            pltpu.SemaphoreType.DMA((steps,)),
            pltpu.SemaphoreType.DMA,
        ],
        compiler_params=pltpu.CompilerParams(vmem_limit_bytes=24 << 20),
        cost_estimate=pl.CostEstimate(
            flops=4 * frames * frames * held,
            bytes_accessed=4 * frames * held,
            transcendentals=0,
        ),
    )(in_hbm(series), in_hbm(noise_mask.reshape(1, voxels)), probes.T, before)


def note_owners(plan, tile_owner, inverse):
    for residue in range(plan.devices):
        inverse[tile_owner[residue]] = residue


def add_tiles(plan, stage, inverse, sources, place, slot, height, skip=0, rows=None):
    rows = height if rows is None else rows
    device = lax.axis_index(AXIS)
    done, after = plan.done[stage], plan.done[stage + 1]
    slots, devices, tiles = plan.slots[stage], plan.devices, plan.tiles
    residue = inverse[device ^ plan.relative(place, stage + 1)]
    last = stage + 1 == len(plan.widths)
    base = 0 if last else ((device >> after) << after) * plan.owned
    tile = (base + ((residue - base) & (devices - 1)) + slot * devices) & (tiles - 1)
    total = None
    for digit, source in enumerate(sources):
        sender = device ^ (digit << done)
        first = ((sender >> done) << done) * plan.owned
        offset = (tile - first) & (tiles - 1)
        there = offset < slots * devices
        at = place * slots + jnp.minimum(offset >> plan.log, slots - 1)
        value = source[pl.ds(pl.multiple_of(at * height + skip, 8), rows), :]
        value = jnp.where(there, value, 0.0)
        total = value if total is None else total + value
    return total


def add_coefs(sources):
    total = None
    for source in sources:
        value = source[pl.ds(source.shape[0] - COEF_ROWS, COEF_ROWS), :]
        total = value if total is None else total + value
    return total


def merge_kernel(plan, stage, span, fresh, tile_owner, *refs):
    fan = 1 << plan.widths[stage]
    sources, refs = refs[:fan], refs[fan:]
    coefs = None
    if fresh:
        coefs, refs = refs[0][...] + refs[1][...], refs[2:]
    outs, inverse = refs[:-1], refs[-1]
    begin, rows = span
    slots, count = plan.slots[stage + 1], plan.owners[stage + 1]
    size = count * slots * rows
    note_owners(plan, tile_owner, inverse)
    if outs[0].shape[0] > size:
        if not fresh:
            coefs = add_coefs(sources)
        for out in outs:
            out[pl.ds(size, COEF_ROWS), :] = coefs
    height, skip = (plan.frames, begin) if stage == 0 else (rows, 0)
    for digit, out in enumerate(outs):

        def owner(rest, carry):
            for slot in range(slots):
                value = add_tiles(
                    plan, stage, inverse, sources, digit * count + rest, slot,
                    height, skip, rows,
                )
                target = pl.ds(pl.multiple_of((rest * slots + slot) * rows, 8), rows)
                out[target, :] = value
            return carry

        if count <= 4:
            for rest in range(count):
                owner(rest, 0)
        else:
            lax.fori_loop(0, count, owner, 0)


def merge(plan, stage, span, riding, tile_owner, sources, coefs=()):
    fan = 1 << plan.widths[stage + 1]
    rows = plan.tiles_in(stage + 1) * span[1] + (COEF_ROWS if riding else 0)
    block = jax.ShapeDtypeStruct((rows, LANES), jnp.float32)
    vmem = pl.BlockSpec(memory_space=pltpu.VMEM)
    arrays = list(sources) + list(coefs)
    return pl.pallas_call(
        functools.partial(merge_kernel, plan, stage, span, len(coefs) > 0),
        name="merge",
        in_specs=[pl.BlockSpec(memory_space=pltpu.SMEM)] + [vmem] * len(arrays),
        out_specs=[vmem] * fan,
        out_shape=[block] * fan,
        scratch_shapes=[pltpu.SMEM((plan.devices,), jnp.int32)],
        compiler_params=pltpu.CompilerParams(vmem_limit_bytes=32 << 20),
    )(tile_owner, *arrays)


def finish_kernel(plan, comps, spans, tile_owner, *refs):
    stage = len(plan.widths) - 1
    fan = 1 << plan.widths[stage]
    parts = [refs[i * fan : (i + 1) * fan] for i in range(len(spans))]
    out, inverse = refs[-2:]
    frames = plan.frames
    note_owners(plan, tile_owner, inverse)
    basis = add_coefs(parts[-1])
    lane = lax.broadcasted_iota(jnp.int32, basis.shape, 1)
    row = lax.broadcasted_iota(jnp.int32, basis.shape, 0)
    basis = jnp.where((lane < frames) & (row < comps), basis, 0.0)
    unit = jnp.zeros_like(basis)
    for i in range(comps):
        line = basis[i : i + 1, :]
        dots = jnp.sum(basis * line, axis=1, keepdims=True)
        square = dots[i : i + 1, :]
        unit = jnp.where(row == i, line * lax.rsqrt(square), unit)
        basis = basis - dots * (line / square)
    unit = unit[:, 0:frames]
    values = []
    for slot in range(plan.owned):
        pieces = [
            add_tiles(plan, stage, inverse, sources, 0, slot, rows)
            for (begin, rows), sources in zip(spans, parts)
        ]
        values.append(jnp.concatenate(pieces, axis=0))
    value = jnp.concatenate(values, axis=1)
    along = jnp.dot(unit, value, precision=HIGHEST, preferred_element_type=jnp.float32)
    value = value - lax.dot_general(
        unit,
        along,
        (((0,), (0,)), ((), ())),
        precision=HIGHEST,
        preferred_element_type=jnp.float32,
    )
    for slot in range(plan.owned):
        out[slot] = value[:, slot * plan.tile_width : (slot + 1) * plan.tile_width]


def finish(plan, comps, spans, tile_owner, parts):
    vmem = pl.BlockSpec(memory_space=pltpu.VMEM)
    arrays = [block for part in parts for block in part]
    return pl.pallas_call(
        functools.partial(finish_kernel, plan, comps, spans),
        name="finish",
        in_specs=[pl.BlockSpec(memory_space=pltpu.SMEM)] + [vmem] * len(arrays),
        out_specs=vmem,
        out_shape=jax.ShapeDtypeStruct((plan.owned, plan.frames, plan.tile_width), jnp.float32),
        scratch_shapes=[pltpu.SMEM((plan.devices,), jnp.int32)],
        compiler_params=pltpu.CompilerParams(vmem_limit_bytes=32 << 20),
    )(tile_owner, *arrays)


def exchange(plan, stage, blocks):
    received = [blocks[0]]
    for digit in range(1, len(blocks)):
        pairs = [(i, i ^ (digit << plan.done[stage])) for i in range(plan.devices)]
        received.append(lax.ppermute(blocks[digit], AXIS, pairs))
    return received


def body(series, noise_mask, probes, sample_weights, block_ids, tile_ids, tile_owner):
    frames, voxels = series.shape
    entries, block_width, tile_width = sample_weights.shape
    plan = Plan(
        lax.axis_size(AXIS), tile_owner.shape[0], entries, frames, block_width, tile_width
    )
    stages = len(plan.widths)
    rows = frames // CHUNKS
    spans = [(i * rows, rows) for i in range(CHUNKS)]
    steps = voxels // COEF_STEP
    keep, send = sample(plan, series, sample_weights, block_ids, tile_ids, tile_owner)
    keep, send, probes = lax.optimization_barrier((keep, send, probes))
    pair = exchange(plan, 0, [keep, send])
    coefs = jnp.zeros((COEF_ROWS, LANES), jnp.float32)
    coefs = local_coefs(series, noise_mask, probes, coefs, 0, EARLY)
    chunks = [merge(plan, 0, span, False, tile_owner, pair) for span in spans[:-1]]
    chunks[-1], coefs = lax.optimization_barrier((chunks[-1], coefs))
    coefs = local_coefs(series, noise_mask, probes, coefs, EARLY, steps - EARLY)
    coefs = exchange(plan, 0, [coefs, coefs])
    chunks.append(merge(plan, 0, spans[-1], True, tile_owner, pair, coefs))
    for stage in range(1, stages):
        for i, span in enumerate(spans):
            if stage + 1 == stages and i > 0:
                far, chunks[i] = lax.optimization_barrier((chunks[i - 1][2:], chunks[i]))
                chunks[i - 1] = chunks[i - 1][:2] + far
            chunks[i] = exchange(plan, stage, chunks[i])
            if stage + 1 < stages:
                riding = i + 1 == len(spans)
                chunks[i] = merge(plan, stage, span, riding, tile_owner, chunks[i])
    return finish(plan, probes.shape[1], spans, tile_owner, chunks)


def solution(mesh):
    return jax.shard_map(
        body,
        mesh=mesh,
        in_specs=(
            P(None, AXIS),
            P(AXIS),
            P(),
            P(AXIS, None, None),
            P(AXIS),
            P(AXIS),
            P(),
        ),
        out_specs=P(AXIS, None, None),
        check_vma=False,
    )
```

```python
import functools

import jax
import jax.numpy as jnp
from jax import lax
from jax.experimental import pallas as pl
from jax.experimental.pallas import tpu as pltpu
from jax.sharding import PartitionSpec as P

AXIS = "slab"
HIGHEST = lax.Precision.HIGHEST
LANES = 128
COEF_ROWS = 8
GROUP = 8
AHEAD = 3
WIDE = 256
COEF_STEP = 4096
EARLY = 3


class Plan:
    def __init__(self, devices, tiles, entries, frames, block_width, tile_width):
        self.devices = devices
        self.tiles = tiles
        self.entries = entries
        self.frames = frames
        self.block_width = block_width
        self.tile_width = tile_width
        self.owned = tiles // devices
        self.log = devices.bit_length() - 1
        assert 1 << self.log == devices and self.owned * devices == tiles
        widths = [1]
        while sum(widths) < self.log:
            widths.append(min(2, self.log - sum(widths)))
        self.widths = widths
        self.done = [sum(widths[:i]) for i in range(len(widths) + 1)]
        self.slots = [
            min(self.owned, -(-(self.owned * (1 << b) + entries - 1) // devices))
            for b in self.done
        ]
        self.slots[-1] = self.owned
        self.owners = [devices >> self.done[i + 1] for i in range(len(widths))]

    def tiles_in(self, stage):
        return self.owners[stage] * self.slots[stage]

    def position(self, rel, stage):
        place = 0
        for i in range(stage, len(self.widths)):
            digit = (rel >> self.done[i]) & ((1 << self.widths[i]) - 1)
            place = (place << self.widths[i]) | digit
        return place

    def relative(self, place, stage):
        rel = 0
        for i in reversed(range(stage, len(self.widths))):
            rel = rel | ((place & ((1 << self.widths[i]) - 1)) << self.done[i])
            place = place >> self.widths[i]
        return rel


def tile_rows(index, frames):
    return pl.ds(pl.multiple_of(index * frames, 8), frames)


def split(values):
    high = values.astype(jnp.bfloat16)
    low = (values - high.astype(jnp.float32)).astype(jnp.bfloat16)
    return high, low


def demean(values):
    return values - jnp.sum(values, axis=0, keepdims=True) * (1.0 / values.shape[0])


def in_hbm(array):
    return pltpu.with_memory_space_constraint(array, pltpu.HBM)


def sample_kernel(
    plan, block_ids, tile_ids, tile_owner, series, weights,
    keep, send, picked, held, pick_sems, weight_sems,
):
    frames, width = plan.frames, plan.block_width
    groups = plan.entries // GROUP

    def pick(k):
        start = pl.multiple_of(block_ids[k] * width, width)
        return pltpu.make_async_copy(
            series.at[:, pl.ds(start, width)], picked.at[k], pick_sems.at[k]
        )

    def fetch(g):
        span = pl.ds(g * GROUP, GROUP)
        return pltpu.make_async_copy(weights.at[span], held.at[span], weight_sems.at[g])

    def begin(g, carry):
        fetch(g).start()
        for i in range(GROUP):
            pick(g * GROUP + i).start()
        return carry

    lax.fori_loop(0, groups, begin, 0)
    keep[...] = jnp.zeros_like(keep)
    send[...] = jnp.zeros_like(send)
    device = lax.axis_index(AXIS)
    spare = plan.owners[0] * plan.slots[0]

    def group(g, carry):
        fetch(g).wait()
        for i in range(GROUP):
            pick(g * GROUP + i).wait()
        for i in range(GROUP):
            k = g * GROUP + i
            tile = tile_ids[k]
            high, low = split(demean(picked[k]))
            both = jnp.dot(
                jnp.concatenate([high, low], axis=0),
                held[k],
                preferred_element_type=jnp.float32,
            )
            total = both[0:frames] + both[frames:]
            rel = tile_owner[tile & (plan.devices - 1)] ^ device
            offset = (tile - device * plan.owned) & (plan.tiles - 1)
            slot = plan.position(rel, 1) * plan.slots[0] + (offset >> plan.log)
            mine = (rel & 1) == 0
            used = tile >= 0
            to_keep = jnp.where(used & mine, slot, spare)
            to_send = jnp.where(used & jnp.logical_not(mine), slot, spare)
            keep[tile_rows(to_keep, frames), :] = total
            send[tile_rows(to_send, frames), :] = total
        return carry

    lax.fori_loop(0, groups, group, 0)


def sample(plan, series, weights, block_ids, tile_ids, tile_owner):
    frames, width = plan.frames, plan.block_width
    smem = pl.BlockSpec(memory_space=pltpu.SMEM)
    vmem = pl.BlockSpec(memory_space=pltpu.VMEM)
    hbm = pl.BlockSpec(memory_space=pl.ANY)
    block = jax.ShapeDtypeStruct(((plan.tiles_in(0) + 1) * frames, LANES), jnp.float32)
    held_bytes = plan.entries * width * (4 * frames + 2 * plan.tile_width)
    return pl.pallas_call(
        functools.partial(sample_kernel, plan),
        name="sample",
        in_specs=[smem, smem, smem, hbm, hbm],
        out_specs=[vmem, vmem],
        out_shape=[block, block],
        scratch_shapes=[
            pltpu.VMEM((plan.entries, frames, width), jnp.float32),
            pltpu.VMEM(weights.shape, weights.dtype),
            pltpu.SemaphoreType.DMA((plan.entries,)),
            pltpu.SemaphoreType.DMA((plan.entries // GROUP,)),
        ],
        compiler_params=pltpu.CompilerParams(
            vmem_limit_bytes=held_bytes + 8 * block.shape[0] * LANES + (6 << 20)
        ),
    )(*[in_hbm(x) for x in (block_ids, tile_ids, tile_owner, series, weights)])


def coef_kernel(
    first, steps, series, mask, probes, before, coefs,
    held, marks, halves, masked, gram, sems, mark_sem,
):
    frames = series.shape[0]
    columns = COEF_STEP

    def fetch(step):
        span = pl.ds(pl.multiple_of(step * columns, columns), columns)
        there = pl.ds(pl.multiple_of((first + step) * columns, columns), columns)
        return pltpu.make_async_copy(series.at[:, there], held.at[:, span], sems.at[step])

    mark_copy = pltpu.make_async_copy(
        mask.at[:, pl.ds(first * columns, steps * columns)], marks, mark_sem
    )
    mark_copy.start()
    for step in range(min(AHEAD, steps)):
        fetch(step).start()
    gram[...] = jnp.zeros_like(gram)
    mark_copy.wait()

    def chunk(step, carry):
        fetch(step).wait()

        @pl.when(step + AHEAD < steps)
        def _():
            fetch(step + AHEAD).start()

        start = step * columns
        for at in range(0, columns, WIDE):
            span = pl.ds(pl.multiple_of(start + at, WIDE), WIDE)
            place = pl.ds(at, WIDE)
            high, low = split(demean(held[:, span]))
            halves[0:frames, place] = high
            halves[frames:, place] = low
            masked[:, place] = high * marks[:, span].astype(jnp.float32).astype(jnp.bfloat16)
        gram[...] += lax.dot_general(
            halves[...],
            masked[...],
            (((1,), (1,)), ((), ())),
            preferred_element_type=jnp.float32,
        )
        return carry

    lax.fori_loop(0, steps, chunk, 0)
    low = gram[frames:, :]
    start = probes[...]
    made = jnp.dot(
        start, gram[0:frames, :] + low, precision=HIGHEST, preferred_element_type=jnp.float32
    ) + lax.dot_general(
        start,
        low,
        (((1,), (1,)), ((), ())),
        precision=HIGHEST,
        preferred_element_type=jnp.float32,
    )
    coefs[...] = before[...]
    coefs[0 : start.shape[0], 0:frames] += made


def local_coefs(series, noise_mask, probes, before, first, steps):
    frames, voxels = series.shape
    held = steps * COEF_STEP
    vmem = pl.BlockSpec(memory_space=pltpu.VMEM)
    hbm = pl.BlockSpec(memory_space=pl.ANY)
    return pl.pallas_call(
        functools.partial(coef_kernel, first, steps),
        name="coefs",
        in_specs=[hbm, hbm, vmem, vmem],
        out_specs=vmem,
        out_shape=jax.ShapeDtypeStruct(before.shape, before.dtype),
        scratch_shapes=[
            pltpu.VMEM((frames, held), series.dtype),
            pltpu.VMEM((1, held), noise_mask.dtype),
            pltpu.VMEM((2 * frames, COEF_STEP), jnp.bfloat16),
            pltpu.VMEM((frames, COEF_STEP), jnp.bfloat16),
            pltpu.VMEM((2 * frames, frames), jnp.float32),
            pltpu.SemaphoreType.DMA((steps,)),
            pltpu.SemaphoreType.DMA,
        ],
        compiler_params=pltpu.CompilerParams(vmem_limit_bytes=24 << 20),
        cost_estimate=pl.CostEstimate(
            flops=4 * frames * frames * held,
            bytes_accessed=4 * frames * held,
            transcendentals=0,
        ),
    )(in_hbm(series), in_hbm(noise_mask.reshape(1, voxels)), probes.T, before)


def note_owners(plan, tile_owner, inverse):
    for residue in range(plan.devices):
        inverse[tile_owner[residue]] = residue


def add_tiles(plan, stage, inverse, sources, place, slot, height, skip=0, rows=None):
    rows = height if rows is None else rows
    device = lax.axis_index(AXIS)
    done, after = plan.done[stage], plan.done[stage + 1]
    slots, devices, tiles = plan.slots[stage], plan.devices, plan.tiles
    residue = inverse[device ^ plan.relative(place, stage + 1)]
    last = stage + 1 == len(plan.widths)
    base = 0 if last else ((device >> after) << after) * plan.owned
    tile = (base + ((residue - base) & (devices - 1)) + slot * devices) & (tiles - 1)
    total = None
    for digit, source in enumerate(sources):
        sender = device ^ (digit << done)
        first = ((sender >> done) << done) * plan.owned
        offset = (tile - first) & (tiles - 1)
        there = offset < slots * devices
        at = place * slots + jnp.minimum(offset >> plan.log, slots - 1)
        value = source[pl.ds(pl.multiple_of(at * height + skip, 8), rows), :]
        value = jnp.where(there, value, 0.0)
        total = value if total is None else total + value
    return total


def add_coefs(sources):
    total = None
    for source in sources:
        value = source[pl.ds(source.shape[0] - COEF_ROWS, COEF_ROWS), :]
        total = value if total is None else total + value
    return total


def merge_kernel(plan, stage, span, fresh, tile_owner, *refs):
    fan = 1 << plan.widths[stage]
    sources, refs = refs[:fan], refs[fan:]
    coefs = None
    if fresh:
        coefs, refs = refs[0][...] + refs[1][...], refs[2:]
    outs, inverse = refs[:-1], refs[-1]
    begin, rows = span
    slots, count = plan.slots[stage + 1], plan.owners[stage + 1]
    size = count * slots * rows
    note_owners(plan, tile_owner, inverse)
    if outs[0].shape[0] > size:
        if not fresh:
            coefs = add_coefs(sources)
        for out in outs:
            out[pl.ds(size, COEF_ROWS), :] = coefs
    height, skip = (plan.frames, begin) if stage == 0 else (rows, 0)
    for digit, out in enumerate(outs):

        def owner(rest, carry):
            for slot in range(slots):
                value = add_tiles(
                    plan, stage, inverse, sources, digit * count + rest, slot,
                    height, skip, rows,
                )
                target = pl.ds(pl.multiple_of((rest * slots + slot) * rows, 8), rows)
                out[target, :] = value
            return carry

        if count <= 4:
            for rest in range(count):
                owner(rest, 0)
        else:
            lax.fori_loop(0, count, owner, 0)


def merge(plan, stage, span, riding, tile_owner, sources, coefs=()):
    fan = 1 << plan.widths[stage + 1]
    rows = plan.tiles_in(stage + 1) * span[1] + (COEF_ROWS if riding else 0)
    block = jax.ShapeDtypeStruct((rows, LANES), jnp.float32)
    vmem = pl.BlockSpec(memory_space=pltpu.VMEM)
    arrays = list(sources) + list(coefs)
    return pl.pallas_call(
        functools.partial(merge_kernel, plan, stage, span, len(coefs) > 0),
        name="merge",
        in_specs=[pl.BlockSpec(memory_space=pltpu.SMEM)] + [vmem] * len(arrays),
        out_specs=[vmem] * fan,
        out_shape=[block] * fan,
        scratch_shapes=[pltpu.SMEM((plan.devices,), jnp.int32)],
        compiler_params=pltpu.CompilerParams(vmem_limit_bytes=32 << 20),
    )(tile_owner, *arrays)


def finish_kernel(plan, comps, spans, tile_owner, *refs):
    stage = len(plan.widths) - 1
    fan = 1 << plan.widths[stage]
    parts = [refs[i * fan : (i + 1) * fan] for i in range(len(spans))]
    out, inverse = refs[-2:]
    frames = plan.frames
    note_owners(plan, tile_owner, inverse)
    basis = add_coefs(parts[-1])
    lane = lax.broadcasted_iota(jnp.int32, basis.shape, 1)
    row = lax.broadcasted_iota(jnp.int32, basis.shape, 0)
    basis = jnp.where((lane < frames) & (row < comps), basis, 0.0)
    unit = jnp.zeros_like(basis)
    for i in range(comps):
        line = basis[i : i + 1, :]
        dots = jnp.sum(basis * line, axis=1, keepdims=True)
        square = dots[i : i + 1, :]
        unit = jnp.where(row == i, line * lax.rsqrt(square), unit)
        basis = basis - dots * (line / square)
    unit = unit[:, 0:frames]
    values = []
    for slot in range(plan.owned):
        pieces = [
            add_tiles(plan, stage, inverse, sources, 0, slot, rows)
            for (begin, rows), sources in zip(spans, parts)
        ]
        values.append(jnp.concatenate(pieces, axis=0))
    value = jnp.concatenate(values, axis=1)
    along = jnp.dot(unit, value, precision=HIGHEST, preferred_element_type=jnp.float32)
    value = value - lax.dot_general(
        unit,
        along,
        (((0,), (0,)), ((), ())),
        precision=HIGHEST,
        preferred_element_type=jnp.float32,
    )
    for slot in range(plan.owned):
        out[slot] = value[:, slot * plan.tile_width : (slot + 1) * plan.tile_width]


def finish(plan, comps, spans, tile_owner, parts):
    vmem = pl.BlockSpec(memory_space=pltpu.VMEM)
    arrays = [block for part in parts for block in part]
    return pl.pallas_call(
        functools.partial(finish_kernel, plan, comps, spans),
        name="finish",
        in_specs=[pl.BlockSpec(memory_space=pltpu.SMEM)] + [vmem] * len(arrays),
        out_specs=vmem,
        out_shape=jax.ShapeDtypeStruct((plan.owned, plan.frames, plan.tile_width), jnp.float32),
        scratch_shapes=[pltpu.SMEM((plan.devices,), jnp.int32)],
        compiler_params=pltpu.CompilerParams(vmem_limit_bytes=32 << 20),
    )(tile_owner, *arrays)


def exchange(plan, stage, blocks):
    received = [blocks[0]]
    for digit in range(1, len(blocks)):
        pairs = [(i, i ^ (digit << plan.done[stage])) for i in range(plan.devices)]
        received.append(lax.ppermute(blocks[digit], AXIS, pairs))
    return received


def body(series, noise_mask, probes, sample_weights, block_ids, tile_ids, tile_owner):
    frames, voxels = series.shape
    entries, block_width, tile_width = sample_weights.shape
    plan = Plan(
        lax.axis_size(AXIS), tile_owner.shape[0], entries, frames, block_width, tile_width
    )
    stages = len(plan.widths)
    cut = frames * 3 // 5 // 8 * 8
    spans = [(0, cut), (cut, frames - cut)]
    steps = voxels // COEF_STEP
    keep, send = sample(plan, series, sample_weights, block_ids, tile_ids, tile_owner)
    keep, send, probes = lax.optimization_barrier((keep, send, probes))
    pair = exchange(plan, 0, [keep, send])
    coefs = jnp.zeros((COEF_ROWS, LANES), jnp.float32)
    coefs = local_coefs(series, noise_mask, probes, coefs, 0, EARLY)
    chunks = [merge(plan, 0, span, False, tile_owner, pair) for span in spans[:-1]]
    chunks[-1], coefs = lax.optimization_barrier((chunks[-1], coefs))
    coefs = local_coefs(series, noise_mask, probes, coefs, EARLY, steps - EARLY)
    coefs = exchange(plan, 0, [coefs, coefs])
    chunks.append(merge(plan, 0, spans[-1], True, tile_owner, pair, coefs))
    for stage in range(1, stages):
        for i, span in enumerate(spans):
            if stage + 1 == stages and i > 0:
                far, near = lax.optimization_barrier((chunks[i - 1][2:], chunks[i][1]))
                chunks[i - 1] = chunks[i - 1][:2] + far
                chunks[i] = [chunks[i][0], near] + list(chunks[i][2:])
            chunks[i] = exchange(plan, stage, chunks[i])
            if stage + 1 < stages:
                riding = i + 1 == len(spans)
                chunks[i] = merge(plan, stage, span, riding, tile_owner, chunks[i])
    return finish(plan, probes.shape[1], spans, tile_owner, chunks)


def solution(mesh):
    return jax.shard_map(
        body,
        mesh=mesh,
        in_specs=(
            P(None, AXIS),
            P(AXIS),
            P(),
            P(AXIS, None, None),
            P(AXIS),
            P(AXIS),
            P(),
        ),
        out_specs=P(AXIS, None, None),
        check_vma=False,
    )
```

```python
import functools

import jax
import jax.numpy as jnp
from jax import lax
from jax.experimental import pallas as pl
from jax.experimental.pallas import tpu as pltpu
from jax.sharding import PartitionSpec as P

AXIS = "slab"
HIGHEST = lax.Precision.HIGHEST
LANES = 128
COEF_ROWS = 8
GROUP = 8
AHEAD = 3
WIDE = 256
COEF_STEP = 4096
EARLY = 4


class Plan:
    def __init__(self, devices, tiles, entries, frames, block_width, tile_width):
        self.devices = devices
        self.tiles = tiles
        self.entries = entries
        self.frames = frames
        self.block_width = block_width
        self.tile_width = tile_width
        self.owned = tiles // devices
        self.log = devices.bit_length() - 1
        assert 1 << self.log == devices and self.owned * devices == tiles
        widths = [1]
        while sum(widths) < self.log:
            widths.append(min(2, self.log - sum(widths)))
        self.widths = widths
        self.done = [sum(widths[:i]) for i in range(len(widths) + 1)]
        self.slots = [
            min(self.owned, -(-(self.owned * (1 << b) + entries - 1) // devices))
            for b in self.done
        ]
        self.slots[-1] = self.owned
        self.owners = [devices >> self.done[i + 1] for i in range(len(widths))]

    def tiles_in(self, stage):
        return self.owners[stage] * self.slots[stage]

    def slot(self, stage, tile, offset):
        return (tile >> self.log) & 1 if self.by_parity(stage) else offset >> self.log

    def by_parity(self, stage):
        return self.slots[stage] == 2 and self.owned % 2 == 0

    def position(self, rel, stage):
        place = 0
        for i in range(stage, len(self.widths)):
            digit = (rel >> self.done[i]) & ((1 << self.widths[i]) - 1)
            place = (place << self.widths[i]) | digit
        return place

    def relative(self, place, stage):
        rel = 0
        for i in reversed(range(stage, len(self.widths))):
            rel = rel | ((place & ((1 << self.widths[i]) - 1)) << self.done[i])
            place = place >> self.widths[i]
        return rel


def tile_rows(index, frames):
    return pl.ds(pl.multiple_of(index * frames, 8), frames)


def split(values):
    high = values.astype(jnp.bfloat16)
    low = (values - high.astype(jnp.float32)).astype(jnp.bfloat16)
    return high, low


def demean(values):
    return values - jnp.sum(values, axis=0, keepdims=True) * (1.0 / values.shape[0])


def in_hbm(array):
    return pltpu.with_memory_space_constraint(array, pltpu.HBM)


def sample_kernel(
    plan, block_ids, tile_ids, tile_owner, series, weights,
    keep, send, picked, held, pick_sems, weight_sems,
):
    frames, width = plan.frames, plan.block_width
    groups = plan.entries // GROUP

    def pick(k):
        start = pl.multiple_of(block_ids[k] * width, width)
        return pltpu.make_async_copy(
            series.at[:, pl.ds(start, width)], picked.at[k], pick_sems.at[k]
        )

    def fetch(g):
        span = pl.ds(g * GROUP, GROUP)
        return pltpu.make_async_copy(weights.at[span], held.at[span], weight_sems.at[g])

    def begin(g, carry):
        fetch(g).start()
        for i in range(GROUP):
            pick(g * GROUP + i).start()
        return carry

    lax.fori_loop(0, groups, begin, 0)
    keep[...] = jnp.zeros_like(keep)
    send[...] = jnp.zeros_like(send)
    device = lax.axis_index(AXIS)
    spare = plan.owners[0] * plan.slots[0]

    def group(g, carry):
        fetch(g).wait()
        for i in range(GROUP):
            pick(g * GROUP + i).wait()
        for i in range(GROUP):
            k = g * GROUP + i
            tile = tile_ids[k]
            high, low = split(demean(picked[k]))
            both = jnp.dot(
                jnp.concatenate([high, low], axis=0),
                held[k],
                preferred_element_type=jnp.float32,
            )
            total = both[0:frames] + both[frames:]
            rel = tile_owner[tile & (plan.devices - 1)] ^ device
            offset = (tile - device * plan.owned) & (plan.tiles - 1)
            slot = plan.position(rel, 1) * plan.slots[0] + plan.slot(0, tile, offset)
            mine = (rel & 1) == 0
            used = tile >= 0
            to_keep = jnp.where(used & mine, slot, spare)
            to_send = jnp.where(used & jnp.logical_not(mine), slot, spare)
            keep[tile_rows(to_keep, frames), :] = total
            send[tile_rows(to_send, frames), :] = total
        return carry

    lax.fori_loop(0, groups, group, 0)


def sample(plan, series, weights, block_ids, tile_ids, tile_owner):
    frames, width = plan.frames, plan.block_width
    smem = pl.BlockSpec(memory_space=pltpu.SMEM)
    vmem = pl.BlockSpec(memory_space=pltpu.VMEM)
    hbm = pl.BlockSpec(memory_space=pl.ANY)
    block = jax.ShapeDtypeStruct(((plan.tiles_in(0) + 1) * frames, LANES), jnp.float32)
    held_bytes = plan.entries * width * (4 * frames + 2 * plan.tile_width)
    return pl.pallas_call(
        functools.partial(sample_kernel, plan),
        name="sample",
        in_specs=[smem, smem, smem, hbm, hbm],
        out_specs=[vmem, vmem],
        out_shape=[block, block],
        scratch_shapes=[
            pltpu.VMEM((plan.entries, frames, width), jnp.float32),
            pltpu.VMEM(weights.shape, weights.dtype),
            pltpu.SemaphoreType.DMA((plan.entries,)),
            pltpu.SemaphoreType.DMA((plan.entries // GROUP,)),
        ],
        compiler_params=pltpu.CompilerParams(
            vmem_limit_bytes=held_bytes + 8 * block.shape[0] * LANES + (6 << 20)
        ),
    )(*[in_hbm(x) for x in (block_ids, tile_ids, tile_owner, series, weights)])


def add_gram(values, marks, halves, masked, gram):
    frames, columns = values.shape
    for at in range(0, columns, WIDE):
        place = pl.ds(at, WIDE)
        high, low = split(demean(values[:, place]))
        halves[0:frames, place] = high
        halves[frames:, place] = low
        masked[:, place] = high * marks[:, place].astype(jnp.float32).astype(jnp.bfloat16)
    gram[...] += lax.dot_general(
        halves[...],
        masked[...],
        (((1,), (1,)), ((), ())),
        preferred_element_type=jnp.float32,
    )


def gram_kernel(first, steps, more, series, mask, *refs):
    columns = COEF_STEP
    if more:
        gram, following, held, marks, halves, masked, sems, mark_sem = refs
        gram[...] = jnp.zeros_like(gram)
    else:
        probes, before, following, coefs = refs[:4]
        held, marks, halves, masked, sems, mark_sem, gram = refs[4:]
        gram[...] = before[...]
        first, steps = first - 1, steps + 1

    def fetch(step):
        span = pl.ds((first + step) * columns, columns)
        target = following if more and step == steps else held.at[step - (not more)]
        return pltpu.make_async_copy(series.at[:, span], target, sems.at[step])

    start = 0 if more else 1
    end = steps + 1 if more else steps
    mark_copy = pltpu.make_async_copy(
        mask.at[:, pl.ds(first * columns, steps * columns)], marks, mark_sem
    )
    mark_copy.start()
    for step in range(start, min(start + AHEAD, end)):
        fetch(step).start()
    mark_copy.wait()
    for step in range(steps):
        values = following
        if step >= start:
            fetch(step).wait()
            values = held.at[step - start]
            if step + AHEAD < end:
                fetch(step + AHEAD).start()
        span = pl.ds(step * columns, columns)
        add_gram(values, marks.at[:, span], halves, masked, gram)
    if more:
        for step in range(max(steps, start), end):
            fetch(step).wait()
        return
    frames = series.shape[0]
    low = gram[frames:, :]
    rows = probes[...]
    made = jnp.dot(
        rows, gram[0:frames, :] + low, precision=HIGHEST, preferred_element_type=jnp.float32
    ) + lax.dot_general(
        rows,
        low,
        (((1,), (1,)), ((), ())),
        precision=HIGHEST,
        preferred_element_type=jnp.float32,
    )
    coefs[...] = jnp.zeros_like(coefs)
    coefs[0 : rows.shape[0], 0:frames] = made


def local_coefs(series, noise_mask, first, steps, probes=None, before=()):
    frames, voxels = series.shape
    more = probes is None
    vmem = pl.BlockSpec(memory_space=pltpu.VMEM)
    hbm = pl.BlockSpec(memory_space=pl.ANY)
    gram = jax.ShapeDtypeStruct((2 * frames, frames), jnp.float32)
    step = jax.ShapeDtypeStruct((frames, COEF_STEP), series.dtype)
    coefs = jax.ShapeDtypeStruct((COEF_ROWS, LANES), jnp.float32)
    arrays = [] if more else [probes.T, *before]
    total = steps if more else steps + 1
    return pl.pallas_call(
        functools.partial(gram_kernel, first, steps, more),
        name="gram" if more else "coefs",
        in_specs=[hbm, hbm] + [vmem] * len(arrays),
        out_specs=[vmem, vmem] if more else vmem,
        out_shape=[gram, step] if more else coefs,
        scratch_shapes=[
            pltpu.VMEM((steps, frames, COEF_STEP), series.dtype),
            pltpu.VMEM((1, total * COEF_STEP), noise_mask.dtype),
            pltpu.VMEM((2 * frames, COEF_STEP), jnp.bfloat16),
            pltpu.VMEM((frames, COEF_STEP), jnp.bfloat16),
            pltpu.SemaphoreType.DMA((steps + 1,)),
            pltpu.SemaphoreType.DMA,
        ]
        + ([] if more else [pltpu.VMEM(gram.shape, gram.dtype)]),
        compiler_params=pltpu.CompilerParams(vmem_limit_bytes=24 << 20),
        cost_estimate=pl.CostEstimate(
            flops=4 * frames * frames * total * COEF_STEP,
            bytes_accessed=4 * frames * total * COEF_STEP,
            transcendentals=0,
        ),
    )(in_hbm(series), in_hbm(noise_mask.reshape(1, voxels)), *arrays)


def note_owners(plan, tile_owner, inverse):
    for residue in range(plan.devices):
        inverse[tile_owner[residue]] = residue


def add_tiles(plan, stage, inverse, sources, place, slot, height, skip=0, rows=None):
    rows = height if rows is None else rows
    device = lax.axis_index(AXIS)
    done, after = plan.done[stage], plan.done[stage + 1]
    slots, devices, tiles = plan.slots[stage], plan.devices, plan.tiles
    residue = inverse[device ^ plan.relative(place, stage + 1)]
    last = stage + 1 == len(plan.widths)
    base = 0 if last else ((device >> after) << after) * plan.owned
    start = base + ((residue - base) & (devices - 1))
    if not last and plan.by_parity(stage + 1):
        slot = (start >> plan.log) + slot & 1
    tile = (start + slot * devices) & (tiles - 1)
    total = None
    for digit, source in enumerate(sources):
        sender = device ^ (digit << done)
        first = ((sender >> done) << done) * plan.owned
        offset = (tile - first) & (tiles - 1)
        there = offset < slots * devices
        at = place * slots + jnp.minimum(plan.slot(stage, tile, offset), slots - 1)
        value = source[pl.ds(pl.multiple_of(at * height + skip, 8), rows), :]
        value = jnp.where(there, value, 0.0)
        total = value if total is None else total + value
    return total


def add_coefs(sources):
    total = None
    for source in sources:
        value = source[pl.ds(source.shape[0] - COEF_ROWS, COEF_ROWS), :]
        total = value if total is None else total + value
    return total


def merge_kernel(plan, stage, span, fresh, *refs):
    fan = 1 << plan.widths[stage]
    plain = plan.by_parity(stage) and plan.by_parity(stage + 1)
    if not plain:
        tile_owner, inverse, refs = refs[0], refs[-1], refs[1:-1]
        note_owners(plan, tile_owner, inverse)
    sources, outs = refs[:fan], refs[fan:]
    coefs = None
    if fresh:
        coefs, outs = outs[0][...] + outs[1][...], outs[2:]
    begin, rows = span
    slots, count = plan.slots[stage + 1], plan.owners[stage + 1]
    size = count * slots * rows
    if outs[0].shape[0] > size:
        if not fresh:
            coefs = add_coefs(sources)
        for out in outs:
            out[pl.ds(size, COEF_ROWS), :] = coefs
    height, skip = (plan.frames, begin) if stage == 0 else (rows, 0)
    for digit, out in enumerate(outs):

        def add(i, carry):
            place, slot = digit * count + i // slots, i % slots
            if plain:
                read = pl.ds(pl.multiple_of((place * slots + slot) * height + skip, 8), rows)
                value = sources[0][read, :]
                for source in sources[1:]:
                    value = value + source[read, :]
            else:
                value = add_tiles(
                    plan, stage, inverse, sources, place, slot, height, skip, rows
                )
            out[pl.ds(pl.multiple_of(i * rows, 8), rows), :] = value
            return carry

        if count <= 4:
            for i in range(count * slots):
                add(i, 0)
        else:
            lax.fori_loop(0, count * slots, add, 0)


def merge(plan, stage, span, riding, tile_owner, sources, coefs=()):
    fan = 1 << plan.widths[stage + 1]
    rows = plan.tiles_in(stage + 1) * span[1] + (COEF_ROWS if riding else 0)
    block = jax.ShapeDtypeStruct((rows, LANES), jnp.float32)
    vmem = pl.BlockSpec(memory_space=pltpu.VMEM)
    arrays = list(sources) + list(coefs)
    specs, scratch = [vmem] * len(arrays), []
    if not (plan.by_parity(stage) and plan.by_parity(stage + 1)):
        arrays, specs = [tile_owner] + arrays, [pl.BlockSpec(memory_space=pltpu.SMEM)] + specs
        scratch = [pltpu.SMEM((plan.devices,), jnp.int32)]
    return pl.pallas_call(
        functools.partial(merge_kernel, plan, stage, span, len(coefs) > 0),
        name="merge",
        in_specs=specs,
        out_specs=[vmem] * fan,
        out_shape=[block] * fan,
        scratch_shapes=scratch,
        compiler_params=pltpu.CompilerParams(vmem_limit_bytes=32 << 20),
    )(*arrays)


def finish_kernel(plan, comps, spans, tile_owner, *refs):
    stage = len(plan.widths) - 1
    fan = 1 << plan.widths[stage]
    parts = [refs[i * fan : (i + 1) * fan] for i in range(len(spans))]
    out, inverse = refs[-2:]
    frames = plan.frames
    note_owners(plan, tile_owner, inverse)
    basis = add_coefs(parts[-1])
    lane = lax.broadcasted_iota(jnp.int32, basis.shape, 1)
    row = lax.broadcasted_iota(jnp.int32, basis.shape, 0)
    basis = jnp.where((lane < frames) & (row < comps), basis, 0.0)
    unit = jnp.zeros_like(basis)
    for i in range(comps):
        line = basis[i : i + 1, :]
        dots = jnp.sum(basis * line, axis=1, keepdims=True)
        square = dots[i : i + 1, :]
        unit = jnp.where(row == i, line * lax.rsqrt(square), unit)
        basis = basis - dots * (line / square)
    unit = unit[:, 0:frames]
    values = []
    for slot in range(plan.owned):
        pieces = [
            add_tiles(plan, stage, inverse, sources, 0, slot, rows)
            for (begin, rows), sources in zip(spans, parts)
        ]
        values.append(jnp.concatenate(pieces, axis=0))
    value = jnp.concatenate(values, axis=1)
    unit_high, unit_low = split(unit)
    high, low = split(value)
    wide = jnp.concatenate([unit_high, unit_low, unit_high], axis=1)
    along = jnp.dot(
        wide, jnp.concatenate([high, high, low], axis=0), preferred_element_type=jnp.float32
    )
    high, low = split(along)
    tall = jnp.concatenate([unit_high, unit_low, unit_high], axis=0)
    value = value - lax.dot_general(
        tall,
        jnp.concatenate([high, high, low], axis=0),
        (((0,), (0,)), ((), ())),
        preferred_element_type=jnp.float32,
    )
    for slot in range(plan.owned):
        out[slot] = value[:, slot * plan.tile_width : (slot + 1) * plan.tile_width]


def finish(plan, comps, spans, tile_owner, parts):
    vmem = pl.BlockSpec(memory_space=pltpu.VMEM)
    arrays = [block for part in parts for block in part]
    return pl.pallas_call(
        functools.partial(finish_kernel, plan, comps, spans),
        name="finish",
        in_specs=[pl.BlockSpec(memory_space=pltpu.SMEM)] + [vmem] * len(arrays),
        out_specs=vmem,
        out_shape=jax.ShapeDtypeStruct((plan.owned, plan.frames, plan.tile_width), jnp.float32),
        scratch_shapes=[pltpu.SMEM((plan.devices,), jnp.int32)],
        compiler_params=pltpu.CompilerParams(vmem_limit_bytes=32 << 20),
    )(tile_owner, *arrays)


def exchange(plan, stage, blocks):
    received = [blocks[0]]
    for digit in range(1, len(blocks)):
        pairs = [(i, i ^ (digit << plan.done[stage])) for i in range(plan.devices)]
        received.append(lax.ppermute(blocks[digit], AXIS, pairs))
    return received


def body(series, noise_mask, probes, sample_weights, block_ids, tile_ids, tile_owner):
    frames, voxels = series.shape
    entries, block_width, tile_width = sample_weights.shape
    plan = Plan(
        lax.axis_size(AXIS), tile_owner.shape[0], entries, frames, block_width, tile_width
    )
    stages = len(plan.widths)
    cut = frames * 3 // 5 // 8 * 8
    spans = [(0, cut), (cut, frames - cut)]
    steps = voxels // COEF_STEP
    keep, send = sample(plan, series, sample_weights, block_ids, tile_ids, tile_owner)
    keep, send, marks = lax.optimization_barrier((keep, send, noise_mask))
    pair = exchange(plan, 0, [keep, send])
    grams = local_coefs(series, marks, 0, EARLY)
    chunks = [merge(plan, 0, span, False, tile_owner, pair) for span in spans[:-1]]
    chunks[-1], grams = lax.optimization_barrier((chunks[-1], grams))
    coefs = local_coefs(series, noise_mask, EARLY + 1, steps - EARLY - 1, probes, grams)
    coefs = exchange(plan, 0, [coefs, coefs])
    chunks.append(merge(plan, 0, spans[-1], True, tile_owner, pair, coefs))
    for stage in range(1, stages):
        for i, span in enumerate(spans):
            if stage + 1 == stages and i > 0:
                far, near = lax.optimization_barrier((chunks[i - 1][2:], chunks[i][1]))
                chunks[i - 1] = chunks[i - 1][:2] + far
                chunks[i] = [chunks[i][0], near] + list(chunks[i][2:])
            chunks[i] = exchange(plan, stage, chunks[i])
            if stage + 1 < stages:
                riding = i + 1 == len(spans)
                chunks[i] = merge(plan, stage, span, riding, tile_owner, chunks[i])
    return finish(plan, probes.shape[1], spans, tile_owner, chunks)


def solution(mesh):
    return jax.shard_map(
        body,
        mesh=mesh,
        in_specs=(
            P(None, AXIS),
            P(AXIS),
            P(),
            P(AXIS, None, None),
            P(AXIS),
            P(AXIS),
            P(),
        ),
        out_specs=P(AXIS, None, None),
        check_vma=False,
    )
```

```python
import functools

import jax
import jax.numpy as jnp
from jax import lax
from jax.experimental import pallas as pl
from jax.experimental.pallas import tpu as pltpu
from jax.sharding import PartitionSpec as P

AXIS = "slab"
HIGHEST = lax.Precision.HIGHEST
LANES = 128
COEF_ROWS = 8
GROUP = 8
AHEAD = 3
WIDE = 256
COEF_STEP = 4096
EARLY = 4


class Plan:
    def __init__(self, devices, tiles, entries, frames, block_width, tile_width):
        self.devices = devices
        self.tiles = tiles
        self.entries = entries
        self.frames = frames
        self.block_width = block_width
        self.tile_width = tile_width
        self.owned = tiles // devices
        self.log = devices.bit_length() - 1
        assert 1 << self.log == devices and self.owned * devices == tiles
        widths = [1]
        while sum(widths) < self.log:
            widths.append(min(2, self.log - sum(widths)))
        self.widths = widths
        self.done = [sum(widths[:i]) for i in range(len(widths) + 1)]
        self.slots = [
            min(self.owned, -(-(self.owned * (1 << b) + entries - 1) // devices))
            for b in self.done
        ]
        self.slots[-1] = self.owned
        self.owners = [devices >> self.done[i + 1] for i in range(len(widths))]

    def tiles_in(self, stage):
        return self.owners[stage] * self.slots[stage]

    def slot(self, stage, tile, offset):
        return (tile >> self.log) & 1 if self.by_parity(stage) else offset >> self.log

    def by_parity(self, stage):
        return self.slots[stage] == 2 and self.owned % 2 == 0

    def position(self, rel, stage):
        place = 0
        for i in range(stage, len(self.widths)):
            digit = (rel >> self.done[i]) & ((1 << self.widths[i]) - 1)
            place = (place << self.widths[i]) | digit
        return place

    def relative(self, place, stage):
        rel = 0
        for i in reversed(range(stage, len(self.widths))):
            rel = rel | ((place & ((1 << self.widths[i]) - 1)) << self.done[i])
            place = place >> self.widths[i]
        return rel


def tile_rows(index, frames):
    return pl.ds(pl.multiple_of(index * frames, 8), frames)


def split(values):
    high = values.astype(jnp.bfloat16)
    low = (values - high.astype(jnp.float32)).astype(jnp.bfloat16)
    return high, low


def demean(values):
    return values - jnp.sum(values, axis=0, keepdims=True) * (1.0 / values.shape[0])


def in_hbm(array):
    return pltpu.with_memory_space_constraint(array, pltpu.HBM)


def sample_kernel(
    plan, block_ids, tile_ids, tile_owner, series, weights,
    keep, send, residues, picked, held, inverse, pick_sems, weight_sems,
):
    frames, width = plan.frames, plan.block_width
    groups = plan.entries // GROUP

    def pick(k):
        start = pl.multiple_of(block_ids[k] * width, width)
        return pltpu.make_async_copy(
            series.at[:, pl.ds(start, width)], picked.at[k], pick_sems.at[k]
        )

    def fetch(g):
        span = pl.ds(g * GROUP, GROUP)
        return pltpu.make_async_copy(weights.at[span], held.at[span], weight_sems.at[g])

    def begin(g, carry):
        fetch(g).start()
        for i in range(GROUP):
            pick(g * GROUP + i).start()
        return carry

    lax.fori_loop(0, groups, begin, 0)
    keep[...] = jnp.zeros_like(keep)
    send[...] = jnp.zeros_like(send)
    device = lax.axis_index(AXIS)
    for residue in range(plan.devices):
        inverse[tile_owner[residue]] = residue
    for place in range(residues.shape[0]):
        own = inverse[device ^ plan.relative(place, len(plan.widths) - 1)]
        residues[place] = jnp.full(residues.shape[1:], own, jnp.int32)
    spare = plan.owners[0] * plan.slots[0]

    def group(g, carry):
        fetch(g).wait()
        for i in range(GROUP):
            pick(g * GROUP + i).wait()
        for i in range(GROUP):
            k = g * GROUP + i
            tile = tile_ids[k]
            high, low = split(demean(picked[k]))
            both = jnp.dot(
                jnp.concatenate([high, low], axis=0),
                held[k],
                preferred_element_type=jnp.float32,
            )
            total = both[0:frames] + both[frames:]
            rel = tile_owner[tile & (plan.devices - 1)] ^ device
            offset = (tile - device * plan.owned) & (plan.tiles - 1)
            slot = plan.position(rel, 1) * plan.slots[0] + plan.slot(0, tile, offset)
            mine = (rel & 1) == 0
            used = tile >= 0
            to_keep = jnp.where(used & mine, slot, spare)
            to_send = jnp.where(used & jnp.logical_not(mine), slot, spare)
            keep[tile_rows(to_keep, frames), :] = total
            send[tile_rows(to_send, frames), :] = total
        return carry

    lax.fori_loop(0, groups, group, 0)


def sample(plan, series, weights, block_ids, tile_ids, tile_owner):
    frames, width = plan.frames, plan.block_width
    smem = pl.BlockSpec(memory_space=pltpu.SMEM)
    vmem = pl.BlockSpec(memory_space=pltpu.VMEM)
    hbm = pl.BlockSpec(memory_space=pl.ANY)
    block = jax.ShapeDtypeStruct(((plan.tiles_in(0) + 1) * frames, LANES), jnp.float32)
    held_bytes = plan.entries * width * (4 * frames + 2 * plan.tile_width)
    return pl.pallas_call(
        functools.partial(sample_kernel, plan),
        name="sample",
        in_specs=[smem, smem, smem, hbm, hbm],
        out_specs=[vmem, vmem, vmem],
        out_shape=[
            block,
            block,
            jax.ShapeDtypeStruct((plan.owners[-2], 8, LANES), jnp.int32),
        ],
        scratch_shapes=[
            pltpu.VMEM((plan.entries, frames, width), jnp.float32),
            pltpu.VMEM(weights.shape, weights.dtype),
            pltpu.SMEM((plan.devices,), jnp.int32),
            pltpu.SemaphoreType.DMA((plan.entries,)),
            pltpu.SemaphoreType.DMA((plan.entries // GROUP,)),
        ],
        compiler_params=pltpu.CompilerParams(
            vmem_limit_bytes=held_bytes + 8 * block.shape[0] * LANES + (6 << 20)
        ),
    )(*[in_hbm(x) for x in (block_ids, tile_ids, tile_owner, series, weights)])


def add_gram(values, marks, halves, masked, gram):
    frames, columns = values.shape
    for at in range(0, columns, WIDE):
        place = pl.ds(at, WIDE)
        high, low = split(demean(values[:, place]))
        halves[0:frames, place] = high
        halves[frames:, place] = low
        masked[:, place] = high * marks[:, place].astype(jnp.float32).astype(jnp.bfloat16)
    gram[...] += lax.dot_general(
        halves[...],
        masked[...],
        (((1,), (1,)), ((), ())),
        preferred_element_type=jnp.float32,
    )


def gram_kernel(first, steps, more, series, mask, *refs):
    columns = COEF_STEP
    if more:
        gram, following, held, marks, halves, masked, sems, mark_sem = refs
        gram[...] = jnp.zeros_like(gram)
    else:
        probes, before, following, coefs = refs[:4]
        held, marks, halves, masked, sems, mark_sem, gram = refs[4:]
        gram[...] = before[...]
        first, steps = first - 1, steps + 1

    def fetch(step):
        span = pl.ds((first + step) * columns, columns)
        target = following if more and step == steps else held.at[step - (not more)]
        return pltpu.make_async_copy(series.at[:, span], target, sems.at[step])

    start = 0 if more else 1
    end = steps + 1 if more else steps
    mark_copy = pltpu.make_async_copy(
        mask.at[:, pl.ds(first * columns, steps * columns)], marks, mark_sem
    )
    mark_copy.start()
    for step in range(start, min(start + AHEAD, end)):
        fetch(step).start()
    mark_copy.wait()
    for step in range(steps):
        values = following
        if step >= start:
            fetch(step).wait()
            values = held.at[step - start]
            if step + AHEAD < end:
                fetch(step + AHEAD).start()
        span = pl.ds(step * columns, columns)
        add_gram(values, marks.at[:, span], halves, masked, gram)
    if more:
        for step in range(max(steps, start), end):
            fetch(step).wait()
        return
    frames = series.shape[0]
    low = gram[frames:, :]
    rows = probes[...]
    made = jnp.dot(
        rows, gram[0:frames, :] + low, precision=HIGHEST, preferred_element_type=jnp.float32
    ) + lax.dot_general(
        rows,
        low,
        (((1,), (1,)), ((), ())),
        precision=HIGHEST,
        preferred_element_type=jnp.float32,
    )
    coefs[...] = jnp.zeros_like(coefs)
    coefs[0 : rows.shape[0], 0:frames] = made


def local_coefs(series, noise_mask, first, steps, probes=None, before=()):
    frames, voxels = series.shape
    more = probes is None
    vmem = pl.BlockSpec(memory_space=pltpu.VMEM)
    hbm = pl.BlockSpec(memory_space=pl.ANY)
    gram = jax.ShapeDtypeStruct((2 * frames, frames), jnp.float32)
    step = jax.ShapeDtypeStruct((frames, COEF_STEP), series.dtype)
    coefs = jax.ShapeDtypeStruct((COEF_ROWS, LANES), jnp.float32)
    arrays = [] if more else [probes.T, *before]
    total = steps if more else steps + 1
    return pl.pallas_call(
        functools.partial(gram_kernel, first, steps, more),
        name="gram" if more else "coefs",
        in_specs=[hbm, hbm] + [vmem] * len(arrays),
        out_specs=[vmem, vmem] if more else vmem,
        out_shape=[gram, step] if more else coefs,
        scratch_shapes=[
            pltpu.VMEM((steps, frames, COEF_STEP), series.dtype),
            pltpu.VMEM((1, total * COEF_STEP), noise_mask.dtype),
            pltpu.VMEM((2 * frames, COEF_STEP), jnp.bfloat16),
            pltpu.VMEM((frames, COEF_STEP), jnp.bfloat16),
            pltpu.SemaphoreType.DMA((steps + 1,)),
            pltpu.SemaphoreType.DMA,
        ]
        + ([] if more else [pltpu.VMEM(gram.shape, gram.dtype)]),
        compiler_params=pltpu.CompilerParams(vmem_limit_bytes=24 << 20),
        cost_estimate=pl.CostEstimate(
            flops=4 * frames * frames * total * COEF_STEP,
            bytes_accessed=4 * frames * total * COEF_STEP,
            transcendentals=0,
        ),
    )(in_hbm(series), in_hbm(noise_mask.reshape(1, voxels)), *arrays)


def add_tiles(plan, stage, residue, sources, place, slot, height):
    device = lax.axis_index(AXIS)
    done, after = plan.done[stage], plan.done[stage + 1]
    slots, devices, tiles = plan.slots[stage], plan.devices, plan.tiles
    last = stage + 1 == len(plan.widths)
    base = 0 if last else ((device >> after) << after) * plan.owned
    start = base + ((residue - base) & (devices - 1))
    if not last and plan.by_parity(stage + 1):
        slot = ((start >> plan.log) + slot) & 1
    tile = (start + slot * devices) & (tiles - 1)
    total = [jnp.zeros((8, LANES), jnp.float32)] * (height // 8)
    for digit, source in enumerate(sources):
        sender = device ^ (digit << done)
        first = ((sender >> done) << done) * plan.owned
        offset = (tile - first) & (tiles - 1)
        there = offset < slots * devices
        at = plan.slot(stage, tile, offset)
        for other in range(slots):
            chosen = there & (at == other)
            for i in range(height // 8):
                rows = pl.ds((place * slots + other) * height + 8 * i, 8)
                total[i] = total[i] + jnp.where(chosen, source[rows, :], 0.0)
    return jnp.concatenate(total, axis=0)


def add_coefs(sources):
    total = None
    for source in sources:
        value = source[pl.ds(source.shape[0] - COEF_ROWS, COEF_ROWS), :]
        total = value if total is None else total + value
    return total


def merge_kernel(plan, stage, span, fresh, *refs):
    fan = 1 << plan.widths[stage]
    plain = plan.by_parity(stage) and plan.by_parity(stage + 1)
    if not plain:
        residues, refs = refs[0], refs[1:]
    sources, outs = refs[:fan], refs[fan:]
    coefs = None
    if fresh:
        coefs, outs = outs[0][...] + outs[1][...], outs[2:]
    begin, rows = span
    slots, count = plan.slots[stage + 1], plan.owners[stage + 1]
    size = count * slots * rows
    if outs[0].shape[0] > size:
        if not fresh:
            coefs = add_coefs(sources)
        for out in outs:
            out[pl.ds(size, COEF_ROWS), :] = coefs
    height, skip = (plan.frames, begin) if stage == 0 else (rows, 0)
    assert plain or (skip == 0 and height == rows)
    for digit, out in enumerate(outs):

        def add(i, carry):
            place, slot = digit * count + i // slots, i % slots
            if plain:
                read = pl.ds(pl.multiple_of((place * slots + slot) * height + skip, 8), rows)
                value = sources[0][read, :]
                for source in sources[1:]:
                    value = value + source[read, :]
            else:
                value = add_tiles(plan, stage, residues[place], sources, place, slot, rows)
            out[pl.ds(pl.multiple_of(i * rows, 8), rows), :] = value
            return carry

        if count <= 4 or not plain:
            for i in range(count * slots):
                add(i, 0)
        else:
            lax.fori_loop(0, count * slots, add, 0)


def merge(plan, stage, span, riding, residues, sources, coefs=()):
    fan = 1 << plan.widths[stage + 1]
    rows = plan.tiles_in(stage + 1) * span[1] + (COEF_ROWS if riding else 0)
    block = jax.ShapeDtypeStruct((rows, LANES), jnp.float32)
    vmem = pl.BlockSpec(memory_space=pltpu.VMEM)
    arrays = list(sources) + list(coefs)
    if not (plan.by_parity(stage) and plan.by_parity(stage + 1)):
        assert stage + 2 == len(plan.widths)
        arrays = [residues] + arrays
    return pl.pallas_call(
        functools.partial(merge_kernel, plan, stage, span, len(coefs) > 0),
        name="merge",
        in_specs=[vmem] * len(arrays),
        out_specs=[vmem] * fan,
        out_shape=[block] * fan,
        compiler_params=pltpu.CompilerParams(vmem_limit_bytes=32 << 20),
    )(*arrays)


def finish_kernel(plan, comps, spans, residues, *refs):
    stage = len(plan.widths) - 1
    fan = 1 << plan.widths[stage]
    parts = [refs[i * fan : (i + 1) * fan] for i in range(len(spans))]
    out = refs[-1]
    frames = plan.frames
    basis = add_coefs(parts[-1])
    lane = lax.broadcasted_iota(jnp.int32, basis.shape, 1)
    row = lax.broadcasted_iota(jnp.int32, basis.shape, 0)
    basis = jnp.where((lane < frames) & (row < comps), basis, 0.0)
    unit = jnp.zeros_like(basis)
    for i in range(comps):
        line = basis[i : i + 1, :]
        dots = jnp.sum(basis * line, axis=1, keepdims=True)
        square = dots[i : i + 1, :]
        unit = jnp.where(row == i, line * lax.rsqrt(square), unit)
        basis = basis - dots * (line / square)
    unit = unit[:, 0:frames]
    values = []
    for slot in range(plan.owned):
        pieces = [
            add_tiles(plan, stage, residues[0], sources, 0, slot, rows)
            for (begin, rows), sources in zip(spans, parts)
        ]
        values.append(jnp.concatenate(pieces, axis=0))
    value = jnp.concatenate(values, axis=1)
    unit_high, unit_low = split(unit)
    high, low = split(value)
    wide = jnp.concatenate([unit_high, unit_low, unit_high], axis=1)
    along = jnp.dot(
        wide, jnp.concatenate([high, high, low], axis=0), preferred_element_type=jnp.float32
    )
    high, low = split(along)
    tall = jnp.concatenate([unit_high, unit_low, unit_high], axis=0)
    value = value - lax.dot_general(
        tall,
        jnp.concatenate([high, high, low], axis=0),
        (((0,), (0,)), ((), ())),
        preferred_element_type=jnp.float32,
    )
    for slot in range(plan.owned):
        out[slot] = value[:, slot * plan.tile_width : (slot + 1) * plan.tile_width]


def finish(plan, comps, spans, residues, parts):
    vmem = pl.BlockSpec(memory_space=pltpu.VMEM)
    arrays = [block for part in parts for block in part]
    return pl.pallas_call(
        functools.partial(finish_kernel, plan, comps, spans),
        name="finish",
        in_specs=[vmem] * (1 + len(arrays)),
        out_specs=vmem,
        out_shape=jax.ShapeDtypeStruct((plan.owned, plan.frames, plan.tile_width), jnp.float32),
        compiler_params=pltpu.CompilerParams(vmem_limit_bytes=32 << 20),
    )(residues, *arrays)


def exchange(plan, stage, blocks):
    received = [blocks[0]]
    for digit in range(1, len(blocks)):
        pairs = [(i, i ^ (digit << plan.done[stage])) for i in range(plan.devices)]
        received.append(lax.ppermute(blocks[digit], AXIS, pairs))
    return received


def body(series, noise_mask, probes, sample_weights, block_ids, tile_ids, tile_owner):
    frames, voxels = series.shape
    entries, block_width, tile_width = sample_weights.shape
    plan = Plan(
        lax.axis_size(AXIS), tile_owner.shape[0], entries, frames, block_width, tile_width
    )
    stages = len(plan.widths)
    cut = frames * 3 // 5 // 8 * 8
    spans = [(0, cut), (cut, frames - cut)]
    steps = voxels // COEF_STEP
    keep, send, residues = sample(plan, series, sample_weights, block_ids, tile_ids, tile_owner)
    keep, send, marks = lax.optimization_barrier((keep, send, noise_mask))
    pair = exchange(plan, 0, [keep, send])
    grams = local_coefs(series, marks, 0, EARLY)
    chunks = [merge(plan, 0, span, False, residues, pair) for span in spans[:-1]]
    chunks[-1], grams = lax.optimization_barrier((chunks[-1], grams))
    coefs = local_coefs(series, noise_mask, EARLY + 1, steps - EARLY - 1, probes, grams)
    coefs = exchange(plan, 0, [coefs, coefs])
    chunks.append(merge(plan, 0, spans[-1], True, residues, pair, coefs))
    for stage in range(1, stages):
        for i, span in enumerate(spans):
            if stage + 1 == stages and i > 0:
                far, near = lax.optimization_barrier((chunks[i - 1][2:], chunks[i][1]))
                chunks[i - 1] = chunks[i - 1][:2] + far
                chunks[i] = [chunks[i][0], near] + list(chunks[i][2:])
            chunks[i] = exchange(plan, stage, chunks[i])
            if stage + 1 < stages:
                riding = i + 1 == len(spans)
                chunks[i] = merge(plan, stage, span, riding, residues, chunks[i])
    return finish(plan, probes.shape[1], spans, residues, chunks)


def solution(mesh):
    return jax.shard_map(
        body,
        mesh=mesh,
        in_specs=(
            P(None, AXIS),
            P(AXIS),
            P(),
            P(AXIS, None, None),
            P(AXIS),
            P(AXIS),
            P(),
        ),
        out_specs=P(AXIS, None, None),
        check_vma=False,
    )
```

```python
import functools

import jax
import jax.numpy as jnp
from jax import lax
from jax.experimental import pallas as pl
from jax.experimental.pallas import tpu as pltpu
from jax.sharding import PartitionSpec as P

AXIS = "slab"
HIGHEST = lax.Precision.HIGHEST
LANES = 128
COEF_ROWS = 8
GROUP = 8
AHEAD = 3
WIDE = 256
COEF_STEP = 4096
EARLY = 4


class Plan:
    def __init__(self, devices, tiles, entries, frames, block_width, tile_width):
        self.devices = devices
        self.tiles = tiles
        self.entries = entries
        self.frames = frames
        self.block_width = block_width
        self.tile_width = tile_width
        self.owned = tiles // devices
        self.log = devices.bit_length() - 1
        assert 1 << self.log == devices and self.owned * devices == tiles
        widths = [1]
        while sum(widths) < self.log:
            widths.append(min(2, self.log - sum(widths)))
        self.widths = widths
        self.done = [sum(widths[:i]) for i in range(len(widths) + 1)]
        self.slots = [
            min(self.owned, -(-(self.owned * (1 << b) + entries - 1) // devices))
            for b in self.done
        ]
        self.slots[-1] = self.owned
        self.owners = [devices >> self.done[i + 1] for i in range(len(widths))]

    def tiles_in(self, stage):
        return self.owners[stage] * self.slots[stage]

    def slot(self, stage, tile, offset):
        return (tile >> self.log) & 1 if self.by_parity(stage) else offset >> self.log

    def by_parity(self, stage):
        return self.slots[stage] == 2 and self.owned % 2 == 0

    def position(self, rel, stage):
        place = 0
        for i in range(stage, len(self.widths)):
            digit = (rel >> self.done[i]) & ((1 << self.widths[i]) - 1)
            place = (place << self.widths[i]) | digit
        return place

    def relative(self, place, stage):
        rel = 0
        for i in reversed(range(stage, len(self.widths))):
            rel = rel | ((place & ((1 << self.widths[i]) - 1)) << self.done[i])
            place = place >> self.widths[i]
        return rel


def tile_rows(index, frames):
    return pl.ds(pl.multiple_of(index * frames, 8), frames)


def split(values):
    high = values.astype(jnp.bfloat16)
    low = (values - high.astype(jnp.float32)).astype(jnp.bfloat16)
    return high, low


def demean(values):
    return values - jnp.sum(values, axis=0, keepdims=True) * (1.0 / values.shape[0])


def in_hbm(array):
    return pltpu.with_memory_space_constraint(array, pltpu.HBM)


def sample_kernel(
    plan, block_ids, tile_ids, tile_owner, series, weights,
    keep, send, residues, ahead, picked, held, inverse, pick_sems, weight_sems, sem,
):
    frames, width = plan.frames, plan.block_width
    groups = plan.entries // GROUP

    def pick(k):
        start = pl.multiple_of(block_ids[k] * width, width)
        return pltpu.make_async_copy(
            series.at[:, pl.ds(start, width)], picked.at[k], pick_sems.at[k]
        )

    def fetch(g):
        span = pl.ds(g * GROUP, GROUP)
        return pltpu.make_async_copy(weights.at[span], held.at[span], weight_sems.at[g])

    def begin(g, carry):
        fetch(g).start()
        for i in range(GROUP):
            pick(g * GROUP + i).start()
        return carry

    lax.fori_loop(0, groups, begin, 0)
    ahead_copy = pltpu.make_async_copy(series.at[:, pl.ds(0, COEF_STEP)], ahead, sem)
    ahead_copy.start()
    keep[...] = jnp.zeros_like(keep)
    send[...] = jnp.zeros_like(send)
    device = lax.axis_index(AXIS)
    for residue in range(plan.devices):
        inverse[tile_owner[residue]] = residue
    for place in range(residues.shape[0]):
        own = inverse[device ^ plan.relative(place, len(plan.widths) - 1)]
        residues[place] = jnp.full(residues.shape[1:], own, jnp.int32)
    spare = plan.owners[0] * plan.slots[0]

    def group(g, carry):
        fetch(g).wait()
        for i in range(GROUP):
            pick(g * GROUP + i).wait()
        for i in range(GROUP):
            k = g * GROUP + i
            tile = tile_ids[k]
            high, low = split(demean(picked[k]))
            both = jnp.dot(
                jnp.concatenate([high, low], axis=0),
                held[k],
                preferred_element_type=jnp.float32,
            )
            total = both[0:frames] + both[frames:]
            rel = tile_owner[tile & (plan.devices - 1)] ^ device
            offset = (tile - device * plan.owned) & (plan.tiles - 1)
            slot = plan.position(rel, 1) * plan.slots[0] + plan.slot(0, tile, offset)
            mine = (rel & 1) == 0
            used = tile >= 0
            to_keep = jnp.where(used & mine, slot, spare)
            to_send = jnp.where(used & jnp.logical_not(mine), slot, spare)
            keep[tile_rows(to_keep, frames), :] = total
            send[tile_rows(to_send, frames), :] = total
        return carry

    lax.fori_loop(0, groups, group, 0)
    ahead_copy.wait()


def sample(plan, series, weights, block_ids, tile_ids, tile_owner):
    frames, width = plan.frames, plan.block_width
    smem = pl.BlockSpec(memory_space=pltpu.SMEM)
    vmem = pl.BlockSpec(memory_space=pltpu.VMEM)
    hbm = pl.BlockSpec(memory_space=pl.ANY)
    block = jax.ShapeDtypeStruct(((plan.tiles_in(0) + 1) * frames, LANES), jnp.float32)
    held_bytes = plan.entries * width * (4 * frames + 2 * plan.tile_width)
    return pl.pallas_call(
        functools.partial(sample_kernel, plan),
        name="sample",
        in_specs=[smem, smem, smem, hbm, hbm],
        out_specs=[vmem] * 4,
        out_shape=[
            block,
            block,
            jax.ShapeDtypeStruct((plan.owners[-2], 8, LANES), jnp.int32),
            jax.ShapeDtypeStruct((frames, COEF_STEP), series.dtype),
        ],
        scratch_shapes=[
            pltpu.VMEM((plan.entries, frames, width), jnp.float32),
            pltpu.VMEM(weights.shape, weights.dtype),
            pltpu.SMEM((plan.devices,), jnp.int32),
            pltpu.SemaphoreType.DMA((plan.entries,)),
            pltpu.SemaphoreType.DMA((plan.entries // GROUP,)),
            pltpu.SemaphoreType.DMA,
        ],
        compiler_params=pltpu.CompilerParams(
            vmem_limit_bytes=held_bytes + 8 * block.shape[0] * LANES + (6 << 20)
        ),
    )(*[in_hbm(x) for x in (block_ids, tile_ids, tile_owner, series, weights)])


def add_gram(values, marks, halves, masked, gram):
    frames, columns = values.shape
    for at in range(0, columns, WIDE):
        place = pl.ds(at, WIDE)
        high, low = split(demean(values[:, place]))
        halves[0:frames, place] = high
        halves[frames:, place] = low
        masked[:, place] = high * marks[:, place].astype(jnp.float32).astype(jnp.bfloat16)
    gram[...] += lax.dot_general(
        halves[...],
        masked[...],
        (((1,), (1,)), ((), ())),
        preferred_element_type=jnp.float32,
    )


def gram_kernel(first, steps, more, series, mask, *refs):
    columns = COEF_STEP
    if more:
        here, gram, following, held, marks, halves, masked, sems, mark_sem = refs
        gram[...] = jnp.zeros_like(gram)
    else:
        probes, before, here, coefs = refs[:4]
        held, marks, halves, masked, sems, mark_sem, gram = refs[4:]
        gram[...] = before[...]
        first, steps = first - 1, steps + 1

    def fetch(step):
        span = pl.ds((first + step) * columns, columns)
        target = following if more and step == steps else held.at[step - 1]
        return pltpu.make_async_copy(series.at[:, span], target, sems.at[step])

    start = 1
    end = steps + 1 if more else steps
    mark_copy = pltpu.make_async_copy(
        mask.at[:, pl.ds(first * columns, steps * columns)], marks, mark_sem
    )
    mark_copy.start()
    for step in range(start, min(start + AHEAD, end)):
        fetch(step).start()
    mark_copy.wait()
    for step in range(steps):
        values = here
        if step >= start:
            fetch(step).wait()
            values = held.at[step - start]
            if step + AHEAD < end:
                fetch(step + AHEAD).start()
        span = pl.ds(step * columns, columns)
        add_gram(values, marks.at[:, span], halves, masked, gram)
    if more:
        for step in range(max(steps, start), end):
            fetch(step).wait()
        return
    frames = series.shape[0]
    low = gram[frames:, :]
    rows = probes[...]
    made = jnp.dot(
        rows, gram[0:frames, :] + low, precision=HIGHEST, preferred_element_type=jnp.float32
    ) + lax.dot_general(
        rows,
        low,
        (((1,), (1,)), ((), ())),
        precision=HIGHEST,
        preferred_element_type=jnp.float32,
    )
    coefs[...] = jnp.zeros_like(coefs)
    coefs[0 : rows.shape[0], 0:frames] = made


def local_coefs(series, noise_mask, first, steps, before, probes=None):
    frames, voxels = series.shape
    more = probes is None
    vmem = pl.BlockSpec(memory_space=pltpu.VMEM)
    hbm = pl.BlockSpec(memory_space=pl.ANY)
    gram = jax.ShapeDtypeStruct((2 * frames, frames), jnp.float32)
    step = jax.ShapeDtypeStruct((frames, COEF_STEP), series.dtype)
    coefs = jax.ShapeDtypeStruct((COEF_ROWS, LANES), jnp.float32)
    arrays = [*before] if more else [probes.T, *before]
    total = steps if more else steps + 1
    return pl.pallas_call(
        functools.partial(gram_kernel, first, steps, more),
        name="gram" if more else "coefs",
        in_specs=[hbm, hbm] + [vmem] * len(arrays),
        out_specs=[vmem, vmem] if more else vmem,
        out_shape=[gram, step] if more else coefs,
        scratch_shapes=[
            pltpu.VMEM((total - 1, frames, COEF_STEP), series.dtype),
            pltpu.VMEM((1, total * COEF_STEP), noise_mask.dtype),
            pltpu.VMEM((2 * frames, COEF_STEP), jnp.bfloat16),
            pltpu.VMEM((frames, COEF_STEP), jnp.bfloat16),
            pltpu.SemaphoreType.DMA((steps + 1,)),
            pltpu.SemaphoreType.DMA,
        ]
        + ([] if more else [pltpu.VMEM(gram.shape, gram.dtype)]),
        compiler_params=pltpu.CompilerParams(vmem_limit_bytes=24 << 20),
        cost_estimate=pl.CostEstimate(
            flops=4 * frames * frames * total * COEF_STEP,
            bytes_accessed=4 * frames * total * COEF_STEP,
            transcendentals=0,
        ),
    )(in_hbm(series), in_hbm(noise_mask.reshape(1, voxels)), *arrays)


def add_tiles(plan, stage, residue, sources, place, slot, height):
    device = lax.axis_index(AXIS)
    done, after = plan.done[stage], plan.done[stage + 1]
    slots, devices, tiles = plan.slots[stage], plan.devices, plan.tiles
    last = stage + 1 == len(plan.widths)
    base = 0 if last else ((device >> after) << after) * plan.owned
    start = base + ((residue - base) & (devices - 1))
    if not last and plan.by_parity(stage + 1):
        slot = ((start >> plan.log) + slot) & 1
    tile = (start + slot * devices) & (tiles - 1)
    total = [jnp.zeros((8, LANES), jnp.float32)] * (height // 8)
    for digit, source in enumerate(sources):
        sender = device ^ (digit << done)
        first = ((sender >> done) << done) * plan.owned
        offset = (tile - first) & (tiles - 1)
        there = offset < slots * devices
        at = plan.slot(stage, tile, offset)
        for other in range(slots):
            chosen = there & (at == other)
            for i in range(height // 8):
                rows = pl.ds((place * slots + other) * height + 8 * i, 8)
                total[i] = total[i] + jnp.where(chosen, source[rows, :], 0.0)
    return jnp.concatenate(total, axis=0)


def add_coefs(sources):
    total = None
    for source in sources:
        value = source[pl.ds(source.shape[0] - COEF_ROWS, COEF_ROWS), :]
        total = value if total is None else total + value
    return total


def merge_kernel(plan, stage, span, fresh, *refs):
    fan = 1 << plan.widths[stage]
    plain = plan.by_parity(stage) and plan.by_parity(stage + 1)
    if not plain:
        residues, refs = refs[0], refs[1:]
    sources, outs = refs[:fan], refs[fan:]
    coefs = None
    if fresh:
        coefs, outs = outs[0][...] + outs[1][...], outs[2:]
    begin, rows = span
    slots, count = plan.slots[stage + 1], plan.owners[stage + 1]
    size = count * slots * rows
    if outs[0].shape[0] > size:
        if not fresh:
            coefs = add_coefs(sources)
        for out in outs:
            out[pl.ds(size, COEF_ROWS), :] = coefs
    height, skip = (plan.frames, begin) if stage == 0 else (rows, 0)
    assert plain or (skip == 0 and height == rows)
    for digit, out in enumerate(outs):

        def add(i, carry):
            place, slot = digit * count + i // slots, i % slots
            if plain:
                read = pl.ds(pl.multiple_of((place * slots + slot) * height + skip, 8), rows)
                value = sources[0][read, :]
                for source in sources[1:]:
                    value = value + source[read, :]
            else:
                value = add_tiles(plan, stage, residues[place], sources, place, slot, rows)
            out[pl.ds(pl.multiple_of(i * rows, 8), rows), :] = value
            return carry

        if count <= 4 or not plain:
            for i in range(count * slots):
                add(i, 0)
        else:
            lax.fori_loop(0, count * slots, add, 0)


def merge(plan, stage, span, riding, residues, sources, coefs=()):
    fan = 1 << plan.widths[stage + 1]
    rows = plan.tiles_in(stage + 1) * span[1] + (COEF_ROWS if riding else 0)
    block = jax.ShapeDtypeStruct((rows, LANES), jnp.float32)
    vmem = pl.BlockSpec(memory_space=pltpu.VMEM)
    arrays = list(sources) + list(coefs)
    if not (plan.by_parity(stage) and plan.by_parity(stage + 1)):
        assert stage + 2 == len(plan.widths)
        arrays = [residues] + arrays
    return pl.pallas_call(
        functools.partial(merge_kernel, plan, stage, span, len(coefs) > 0),
        name="merge",
        in_specs=[vmem] * len(arrays),
        out_specs=[vmem] * fan,
        out_shape=[block] * fan,
        compiler_params=pltpu.CompilerParams(vmem_limit_bytes=32 << 20),
    )(*arrays)


def finish_kernel(plan, comps, spans, residues, *refs):
    stage = len(plan.widths) - 1
    fan = 1 << plan.widths[stage]
    parts = [refs[i * fan : (i + 1) * fan] for i in range(len(spans))]
    out = refs[-1]
    frames = plan.frames
    basis = add_coefs(parts[-1])
    lane = lax.broadcasted_iota(jnp.int32, basis.shape, 1)
    row = lax.broadcasted_iota(jnp.int32, basis.shape, 0)
    basis = jnp.where((lane < frames) & (row < comps), basis, 0.0)
    unit = jnp.zeros_like(basis)
    for i in range(comps):
        line = basis[i : i + 1, :]
        dots = jnp.sum(basis * line, axis=1, keepdims=True)
        square = dots[i : i + 1, :]
        unit = jnp.where(row == i, line * lax.rsqrt(square), unit)
        basis = basis - dots * (line / square)
    unit = unit[:, 0:frames]
    values = []
    for slot in range(plan.owned):
        pieces = [
            add_tiles(plan, stage, residues[0], sources, 0, slot, rows)
            for (begin, rows), sources in zip(spans, parts)
        ]
        values.append(jnp.concatenate(pieces, axis=0))
    value = jnp.concatenate(values, axis=1)
    unit_high, unit_low = split(unit)
    high, low = split(value)
    wide = jnp.concatenate([unit_high, unit_low, unit_high], axis=1)
    along = jnp.dot(
        wide, jnp.concatenate([high, high, low], axis=0), preferred_element_type=jnp.float32
    )
    high, low = split(along)
    tall = jnp.concatenate([unit_high, unit_low, unit_high], axis=0)
    value = value - lax.dot_general(
        tall,
        jnp.concatenate([high, high, low], axis=0),
        (((0,), (0,)), ((), ())),
        preferred_element_type=jnp.float32,
    )
    for slot in range(plan.owned):
        out[slot] = value[:, slot * plan.tile_width : (slot + 1) * plan.tile_width]


def finish(plan, comps, spans, residues, parts):
    vmem = pl.BlockSpec(memory_space=pltpu.VMEM)
    arrays = [block for part in parts for block in part]
    return pl.pallas_call(
        functools.partial(finish_kernel, plan, comps, spans),
        name="finish",
        in_specs=[vmem] * (1 + len(arrays)),
        out_specs=vmem,
        out_shape=jax.ShapeDtypeStruct((plan.owned, plan.frames, plan.tile_width), jnp.float32),
        compiler_params=pltpu.CompilerParams(vmem_limit_bytes=32 << 20),
    )(residues, *arrays)


def exchange(plan, stage, blocks):
    received = [blocks[0]]
    for digit in range(1, len(blocks)):
        pairs = [(i, i ^ (digit << plan.done[stage])) for i in range(plan.devices)]
        received.append(lax.ppermute(blocks[digit], AXIS, pairs))
    return received


def body(series, noise_mask, probes, sample_weights, block_ids, tile_ids, tile_owner):
    frames, voxels = series.shape
    entries, block_width, tile_width = sample_weights.shape
    plan = Plan(
        lax.axis_size(AXIS), tile_owner.shape[0], entries, frames, block_width, tile_width
    )
    stages = len(plan.widths)
    cut = frames * 3 // 5 // 8 * 8
    spans = [(0, cut), (cut, frames - cut)]
    steps = voxels // COEF_STEP
    keep, send, residues, ahead = sample(plan, series, sample_weights, block_ids, tile_ids, tile_owner)
    keep, send, marks = lax.optimization_barrier((keep, send, noise_mask))
    pair = exchange(plan, 0, [keep, send])
    grams = local_coefs(series, marks, 0, EARLY, [ahead])
    chunks = [merge(plan, 0, span, False, residues, pair) for span in spans[:-1]]
    chunks[-1], grams = lax.optimization_barrier((chunks[-1], grams))
    coefs = local_coefs(series, noise_mask, EARLY + 1, steps - EARLY - 1, grams, probes)
    coefs = exchange(plan, 0, [coefs, coefs])
    chunks.append(merge(plan, 0, spans[-1], True, residues, pair, coefs))
    for stage in range(1, stages):
        for i, span in enumerate(spans):
            if stage + 1 == stages and i > 0:
                far, near = lax.optimization_barrier((chunks[i - 1][2:], chunks[i][1]))
                chunks[i - 1] = chunks[i - 1][:2] + far
                chunks[i] = [chunks[i][0], near] + list(chunks[i][2:])
            chunks[i] = exchange(plan, stage, chunks[i])
            if stage + 1 < stages:
                riding = i + 1 == len(spans)
                chunks[i] = merge(plan, stage, span, riding, residues, chunks[i])
    return finish(plan, probes.shape[1], spans, residues, chunks)


def solution(mesh):
    return jax.shard_map(
        body,
        mesh=mesh,
        in_specs=(
            P(None, AXIS),
            P(AXIS),
            P(),
            P(AXIS, None, None),
            P(AXIS),
            P(AXIS),
            P(),
        ),
        out_specs=P(AXIS, None, None),
        check_vma=False,
    )
```

```python
import functools

import jax
import jax.numpy as jnp
from jax import lax
from jax.experimental import pallas as pl
from jax.experimental.pallas import tpu as pltpu
from jax.sharding import PartitionSpec as P

AXIS = "slab"
HIGHEST = lax.Precision.HIGHEST
LANES = 128
COEF_ROWS = 8
GROUP = 12
AHEAD = 3
WIDE = 256
COEF_STEP = 4096
EARLY = 4


class Plan:
    def __init__(self, devices, tiles, entries, frames, block_width, tile_width):
        self.devices = devices
        self.tiles = tiles
        self.entries = entries
        self.frames = frames
        self.block_width = block_width
        self.tile_width = tile_width
        self.owned = tiles // devices
        self.log = devices.bit_length() - 1
        assert 1 << self.log == devices and self.owned * devices == tiles
        widths = [1]
        while sum(widths) < self.log:
            widths.append(min(2, self.log - sum(widths)))
        self.widths = widths
        self.done = [sum(widths[:i]) for i in range(len(widths) + 1)]
        self.slots = [
            min(self.owned, -(-(self.owned * (1 << b) + entries - 1) // devices))
            for b in self.done
        ]
        self.slots[-1] = self.owned
        self.owners = [devices >> self.done[i + 1] for i in range(len(widths))]

    def tiles_in(self, stage):
        return self.owners[stage] * self.slots[stage]

    def slot(self, stage, tile, offset):
        return (tile >> self.log) & 1 if self.by_parity(stage) else offset >> self.log

    def by_parity(self, stage):
        return self.slots[stage] == 2 and self.owned % 2 == 0

    def position(self, rel, stage):
        place = 0
        for i in range(stage, len(self.widths)):
            digit = (rel >> self.done[i]) & ((1 << self.widths[i]) - 1)
            place = (place << self.widths[i]) | digit
        return place

    def relative(self, place, stage):
        rel = 0
        for i in reversed(range(stage, len(self.widths))):
            rel = rel | ((place & ((1 << self.widths[i]) - 1)) << self.done[i])
            place = place >> self.widths[i]
        return rel


def tile_rows(index, frames):
    return pl.ds(pl.multiple_of(index * frames, 8), frames)


def split(values):
    high = values.astype(jnp.bfloat16)
    low = (values - high.astype(jnp.float32)).astype(jnp.bfloat16)
    return high, low


def demean(values):
    return values - jnp.sum(values, axis=0, keepdims=True) * (1.0 / values.shape[0])


def in_hbm(array):
    return pltpu.with_memory_space_constraint(array, pltpu.HBM)


def sample_kernel(
    plan, block_ids, tile_ids, tile_owner, series, weights,
    keep, send, residues, ahead, picked, held, inverse, pick_sems, weight_sems, sem,
):
    frames, width = plan.frames, plan.block_width
    groups = plan.entries // GROUP

    def pick(k):
        start = pl.multiple_of(block_ids[k] * width, width)
        return pltpu.make_async_copy(
            series.at[:, pl.ds(start, width)], picked.at[k], pick_sems.at[k]
        )

    def fetch(g):
        span = pl.ds(g * GROUP, GROUP)
        return pltpu.make_async_copy(weights.at[span], held.at[span], weight_sems.at[g])

    def begin(g, carry):
        fetch(g).start()
        for i in range(GROUP):
            pick(g * GROUP + i).start()
        return carry

    lax.fori_loop(0, groups, begin, 0)
    ahead_copy = pltpu.make_async_copy(series.at[:, pl.ds(0, COEF_STEP)], ahead, sem)
    ahead_copy.start()
    keep[...] = jnp.zeros_like(keep)
    send[...] = jnp.zeros_like(send)
    device = lax.axis_index(AXIS)
    for residue in range(plan.devices):
        inverse[tile_owner[residue]] = residue
    for place in range(residues.shape[0]):
        own = inverse[device ^ plan.relative(place, len(plan.widths) - 1)]
        residues[place] = jnp.full(residues.shape[1:], own, jnp.int32)
    spare = plan.owners[0] * plan.slots[0]

    def group(g, carry):
        fetch(g).wait()
        for i in range(GROUP):
            pick(g * GROUP + i).wait()
        for i in range(GROUP):
            k = g * GROUP + i
            tile = tile_ids[k]
            high, low = split(demean(picked[k]))
            both = jnp.dot(
                jnp.concatenate([high, low], axis=0),
                held[k],
                preferred_element_type=jnp.float32,
            )
            total = both[0:frames] + both[frames:]
            rel = tile_owner[tile & (plan.devices - 1)] ^ device
            offset = (tile - device * plan.owned) & (plan.tiles - 1)
            slot = plan.position(rel, 1) * plan.slots[0] + plan.slot(0, tile, offset)
            mine = (rel & 1) == 0
            used = tile >= 0
            to_keep = jnp.where(used & mine, slot, spare)
            to_send = jnp.where(used & jnp.logical_not(mine), slot, spare)
            keep[tile_rows(to_keep, frames), :] = total
            send[tile_rows(to_send, frames), :] = total
        return carry

    lax.fori_loop(0, groups, group, 0)
    ahead_copy.wait()


def sample(plan, series, weights, block_ids, tile_ids, tile_owner):
    frames, width = plan.frames, plan.block_width
    smem = pl.BlockSpec(memory_space=pltpu.SMEM)
    vmem = pl.BlockSpec(memory_space=pltpu.VMEM)
    hbm = pl.BlockSpec(memory_space=pl.ANY)
    block = jax.ShapeDtypeStruct(((plan.tiles_in(0) + 1) * frames, LANES), jnp.float32)
    held_bytes = plan.entries * width * (4 * frames + 2 * plan.tile_width)
    return pl.pallas_call(
        functools.partial(sample_kernel, plan),
        name="sample",
        in_specs=[smem, smem, smem, hbm, hbm],
        out_specs=[vmem] * 4,
        out_shape=[
            block,
            block,
            jax.ShapeDtypeStruct((plan.owners[-2], 8, LANES), jnp.int32),
            jax.ShapeDtypeStruct((frames, COEF_STEP), series.dtype),
        ],
        scratch_shapes=[
            pltpu.VMEM((plan.entries, frames, width), jnp.float32),
            pltpu.VMEM(weights.shape, weights.dtype),
            pltpu.SMEM((plan.devices,), jnp.int32),
            pltpu.SemaphoreType.DMA((plan.entries,)),
            pltpu.SemaphoreType.DMA((plan.entries // GROUP,)),
            pltpu.SemaphoreType.DMA,
        ],
        compiler_params=pltpu.CompilerParams(
            vmem_limit_bytes=held_bytes + 8 * block.shape[0] * LANES + (6 << 20)
        ),
    )(*[in_hbm(x) for x in (block_ids, tile_ids, tile_owner, series, weights)])


def add_gram(values, marks, halves, masked, gram):
    frames, columns = values.shape
    for at in range(0, columns, WIDE):
        place = pl.ds(at, WIDE)
        high, low = split(demean(values[:, place]))
        halves[0:frames, place] = high
        halves[frames:, place] = low
        masked[:, place] = high * marks[:, place].astype(jnp.float32).astype(jnp.bfloat16)
    gram[...] += lax.dot_general(
        halves[...],
        masked[...],
        (((1,), (1,)), ((), ())),
        preferred_element_type=jnp.float32,
    )


def gram_kernel(first, steps, more, series, mask, *refs):
    columns = COEF_STEP
    if more:
        here, gram, following, held, marks, halves, masked, sems, mark_sem = refs
        gram[...] = jnp.zeros_like(gram)
    else:
        probes, before, here, coefs = refs[:4]
        held, marks, halves, masked, sems, mark_sem, gram = refs[4:]
        gram[...] = before[...]
        first, steps = first - 1, steps + 1

    def fetch(step):
        span = pl.ds((first + step) * columns, columns)
        target = following if more and step == steps else held.at[step - 1]
        return pltpu.make_async_copy(series.at[:, span], target, sems.at[step])

    start = 1
    end = steps + 1 if more else steps
    mark_copy = pltpu.make_async_copy(
        mask.at[:, pl.ds(first * columns, steps * columns)], marks, mark_sem
    )
    mark_copy.start()
    for step in range(start, min(start + AHEAD, end)):
        fetch(step).start()
    mark_copy.wait()
    for step in range(steps):
        values = here
        if step >= start:
            fetch(step).wait()
            values = held.at[step - start]
            if step + AHEAD < end:
                fetch(step + AHEAD).start()
        span = pl.ds(step * columns, columns)
        add_gram(values, marks.at[:, span], halves, masked, gram)
    if more:
        for step in range(max(steps, start), end):
            fetch(step).wait()
        return
    frames = series.shape[0]
    low = gram[frames:, :]
    rows = probes[...]
    made = jnp.dot(
        rows, gram[0:frames, :] + low, precision=HIGHEST, preferred_element_type=jnp.float32
    ) + lax.dot_general(
        rows,
        low,
        (((1,), (1,)), ((), ())),
        precision=HIGHEST,
        preferred_element_type=jnp.float32,
    )
    coefs[...] = jnp.zeros_like(coefs)
    coefs[0 : rows.shape[0], 0:frames] = made


def local_coefs(series, noise_mask, first, steps, before, probes=None):
    frames, voxels = series.shape
    more = probes is None
    vmem = pl.BlockSpec(memory_space=pltpu.VMEM)
    hbm = pl.BlockSpec(memory_space=pl.ANY)
    gram = jax.ShapeDtypeStruct((2 * frames, frames), jnp.float32)
    step = jax.ShapeDtypeStruct((frames, COEF_STEP), series.dtype)
    coefs = jax.ShapeDtypeStruct((COEF_ROWS, LANES), jnp.float32)
    arrays = [*before] if more else [probes.T, *before]
    total = steps if more else steps + 1
    return pl.pallas_call(
        functools.partial(gram_kernel, first, steps, more),
        name="gram" if more else "coefs",
        in_specs=[hbm, hbm] + [vmem] * len(arrays),
        out_specs=[vmem, vmem] if more else vmem,
        out_shape=[gram, step] if more else coefs,
        scratch_shapes=[
            pltpu.VMEM((total - 1, frames, COEF_STEP), series.dtype),
            pltpu.VMEM((1, total * COEF_STEP), noise_mask.dtype),
            pltpu.VMEM((2 * frames, COEF_STEP), jnp.bfloat16),
            pltpu.VMEM((frames, COEF_STEP), jnp.bfloat16),
            pltpu.SemaphoreType.DMA((steps + 1,)),
            pltpu.SemaphoreType.DMA,
        ]
        + ([] if more else [pltpu.VMEM(gram.shape, gram.dtype)]),
        compiler_params=pltpu.CompilerParams(vmem_limit_bytes=24 << 20),
        cost_estimate=pl.CostEstimate(
            flops=4 * frames * frames * total * COEF_STEP,
            bytes_accessed=4 * frames * total * COEF_STEP,
            transcendentals=0,
        ),
    )(in_hbm(series), in_hbm(noise_mask.reshape(1, voxels)), *arrays)


def add_tiles(plan, stage, residue, sources, place, slot, height):
    device = lax.axis_index(AXIS)
    done, after = plan.done[stage], plan.done[stage + 1]
    slots, devices, tiles = plan.slots[stage], plan.devices, plan.tiles
    last = stage + 1 == len(plan.widths)
    base = 0 if last else ((device >> after) << after) * plan.owned
    start = base + ((residue - base) & (devices - 1))
    if not last and plan.by_parity(stage + 1):
        slot = ((start >> plan.log) + slot) & 1
    tile = (start + slot * devices) & (tiles - 1)
    total = [jnp.zeros((8, LANES), jnp.float32)] * (height // 8)
    for digit, source in enumerate(sources):
        sender = device ^ (digit << done)
        first = ((sender >> done) << done) * plan.owned
        offset = (tile - first) & (tiles - 1)
        there = offset < slots * devices
        at = plan.slot(stage, tile, offset)
        for other in range(slots):
            chosen = there & (at == other)
            for i in range(height // 8):
                rows = pl.ds((place * slots + other) * height + 8 * i, 8)
                total[i] = total[i] + jnp.where(chosen, source[rows, :], 0.0)
    return jnp.concatenate(total, axis=0)


def add_coefs(sources):
    total = None
    for source in sources:
        value = source[pl.ds(source.shape[0] - COEF_ROWS, COEF_ROWS), :]
        total = value if total is None else total + value
    return total


def merge_kernel(plan, stage, span, fresh, *refs):
    fan = 1 << plan.widths[stage]
    plain = plan.by_parity(stage) and plan.by_parity(stage + 1)
    if not plain:
        residues, refs = refs[0], refs[1:]
    sources, outs = refs[:fan], refs[fan:]
    coefs = None
    if fresh:
        coefs, outs = outs[0][...] + outs[1][...], outs[2:]
    begin, rows = span
    slots, count = plan.slots[stage + 1], plan.owners[stage + 1]
    size = count * slots * rows
    if outs[0].shape[0] > size:
        if not fresh:
            coefs = add_coefs(sources)
        for out in outs:
            out[pl.ds(size, COEF_ROWS), :] = coefs
    height, skip = (plan.frames, begin) if stage == 0 else (rows, 0)
    assert plain or (skip == 0 and height == rows)
    for digit, out in enumerate(outs):

        def add(i, carry):
            place, slot = digit * count + i // slots, i % slots
            if plain:
                read = pl.ds(pl.multiple_of((place * slots + slot) * height + skip, 8), rows)
                value = sources[0][read, :]
                for source in sources[1:]:
                    value = value + source[read, :]
            else:
                value = add_tiles(plan, stage, residues[place], sources, place, slot, rows)
            out[pl.ds(pl.multiple_of(i * rows, 8), rows), :] = value
            return carry

        if count <= 4 or not plain:
            for i in range(count * slots):
                add(i, 0)
        else:
            lax.fori_loop(0, count * slots, add, 0)


def merge(plan, stage, span, riding, residues, sources, coefs=()):
    fan = 1 << plan.widths[stage + 1]
    rows = plan.tiles_in(stage + 1) * span[1] + (COEF_ROWS if riding else 0)
    block = jax.ShapeDtypeStruct((rows, LANES), jnp.float32)
    vmem = pl.BlockSpec(memory_space=pltpu.VMEM)
    arrays = list(sources) + list(coefs)
    if not (plan.by_parity(stage) and plan.by_parity(stage + 1)):
        assert stage + 2 == len(plan.widths)
        arrays = [residues] + arrays
    return pl.pallas_call(
        functools.partial(merge_kernel, plan, stage, span, len(coefs) > 0),
        name="merge",
        in_specs=[vmem] * len(arrays),
        out_specs=[vmem] * fan,
        out_shape=[block] * fan,
        compiler_params=pltpu.CompilerParams(vmem_limit_bytes=32 << 20),
    )(*arrays)


def finish_kernel(plan, comps, spans, residues, *refs):
    stage = len(plan.widths) - 1
    fan = 1 << plan.widths[stage]
    parts = [refs[i * fan : (i + 1) * fan] for i in range(len(spans))]
    out = refs[-1]
    frames = plan.frames
    basis = add_coefs(parts[-1])
    lane = lax.broadcasted_iota(jnp.int32, basis.shape, 1)
    row = lax.broadcasted_iota(jnp.int32, basis.shape, 0)
    basis = jnp.where((lane < frames) & (row < comps), basis, 0.0)
    unit = jnp.zeros_like(basis)
    for i in range(comps):
        line = basis[i : i + 1, :]
        dots = jnp.sum(basis * line, axis=1, keepdims=True)
        square = dots[i : i + 1, :]
        unit = jnp.where(row == i, line * lax.rsqrt(square), unit)
        basis = basis - dots * (line / square)
    unit = unit[:, 0:frames]
    values = []
    for slot in range(plan.owned):
        pieces = [
            add_tiles(plan, stage, residues[0], sources, 0, slot, rows)
            for (begin, rows), sources in zip(spans, parts)
        ]
        values.append(jnp.concatenate(pieces, axis=0))
    value = jnp.concatenate(values, axis=1)
    unit_high, unit_low = split(unit)
    high, low = split(value)
    wide = jnp.concatenate([unit_high, unit_low, unit_high], axis=1)
    along = jnp.dot(
        wide, jnp.concatenate([high, high, low], axis=0), preferred_element_type=jnp.float32
    )
    high, low = split(along)
    tall = jnp.concatenate([unit_high, unit_low, unit_high], axis=0)
    value = value - lax.dot_general(
        tall,
        jnp.concatenate([high, high, low], axis=0),
        (((0,), (0,)), ((), ())),
        preferred_element_type=jnp.float32,
    )
    for slot in range(plan.owned):
        out[slot] = value[:, slot * plan.tile_width : (slot + 1) * plan.tile_width]


def finish(plan, comps, spans, residues, parts):
    vmem = pl.BlockSpec(memory_space=pltpu.VMEM)
    arrays = [block for part in parts for block in part]
    return pl.pallas_call(
        functools.partial(finish_kernel, plan, comps, spans),
        name="finish",
        in_specs=[vmem] * (1 + len(arrays)),
        out_specs=vmem,
        out_shape=jax.ShapeDtypeStruct((plan.owned, plan.frames, plan.tile_width), jnp.float32),
        compiler_params=pltpu.CompilerParams(vmem_limit_bytes=32 << 20),
    )(residues, *arrays)


def exchange(plan, stage, blocks):
    received = [blocks[0]]
    for digit in range(1, len(blocks)):
        pairs = [(i, i ^ (digit << plan.done[stage])) for i in range(plan.devices)]
        received.append(lax.ppermute(blocks[digit], AXIS, pairs))
    return received


def body(series, noise_mask, probes, sample_weights, block_ids, tile_ids, tile_owner):
    frames, voxels = series.shape
    entries, block_width, tile_width = sample_weights.shape
    plan = Plan(
        lax.axis_size(AXIS), tile_owner.shape[0], entries, frames, block_width, tile_width
    )
    stages = len(plan.widths)
    cut = frames * 3 // 5 // 8 * 8
    spans = [(0, cut), (cut, frames - cut)]
    steps = voxels // COEF_STEP
    keep, send, residues, ahead = sample(plan, series, sample_weights, block_ids, tile_ids, tile_owner)
    keep, send, marks = lax.optimization_barrier((keep, send, noise_mask))
    pair = exchange(plan, 0, [keep, send])
    grams = local_coefs(series, marks, 0, EARLY, [ahead])
    chunks = [merge(plan, 0, span, False, residues, pair) for span in spans[:-1]]
    chunks[-1], grams = lax.optimization_barrier((chunks[-1], grams))
    coefs = local_coefs(series, noise_mask, EARLY + 1, steps - EARLY - 1, grams, probes)
    coefs = exchange(plan, 0, [coefs, coefs])
    chunks.append(merge(plan, 0, spans[-1], True, residues, pair, coefs))
    for stage in range(1, stages):
        for i, span in enumerate(spans):
            if stage + 1 == stages and i > 0:
                far, near = lax.optimization_barrier((chunks[i - 1][2:], chunks[i][1]))
                chunks[i - 1] = chunks[i - 1][:2] + far
                chunks[i] = [chunks[i][0], near] + list(chunks[i][2:])
            chunks[i] = exchange(plan, stage, chunks[i])
            if stage + 1 < stages:
                riding = i + 1 == len(spans)
                chunks[i] = merge(plan, stage, span, riding, residues, chunks[i])
    return finish(plan, probes.shape[1], spans, residues, chunks)


def solution(mesh):
    return jax.shard_map(
        body,
        mesh=mesh,
        in_specs=(
            P(None, AXIS),
            P(AXIS),
            P(),
            P(AXIS, None, None),
            P(AXIS),
            P(AXIS),
            P(),
        ),
        out_specs=P(AXIS, None, None),
        check_vma=False,
    )
```
